256 devices in a mesh: mem: 8 (over y, x_lo), grid: 32 (over x_hi, z, core).
Axes of the slice: x: 4 (x_hi: 2, x_lo: 2; x = x_hi * 2 + x_lo), y: 4, z: 8, core: 2. Of those that a mesh axis runs over, the one named last changes fastest.
Arguments:
- initial_concentrations: float32 [32, 4, 768, 1536], P('mem', None, 'grid'), may hold values from 0.5 to 2
- rate_field: bfloat16 [12, 768, 1536], P(None, 'grid'), may hold values from 0.019897461 to 0.29882812
- kinetic_scaling_factors: bfloat16 [32, 12, 256, 6], P('mem', None, 'grid'), may hold values from 0.5 to 2
- observed_cell: int32 [256, 6, 128], P('grid'), may hold values from 0 to 3071
- measured_value: float32 [256, 6, 128], P('grid'), may hold values from 0.5 to 2
- error_variance: float32 [256, 6, 128], P('grid'), may hold values from 0.05 to 0.5
Outputs:
- analysis: bfloat16 [32, 4, 768, 1536], P('mem', None, 'grid')
- mult_analysis: bfloat16 [32, 12, 256, 6], P('mem', None, 'grid')
The draws below stay inside these ranges and needn't reach their ends.
Inputs may be any that keep to these rules, and one draw needn't show every extreme that they name: `observed_cell`: an observation's entry is tracer * 3 * 256 + row * 256 + column within its patch.
All inputs are finite; a program needn't handle non-finite values.
Results may differ from the reference program's by a relative error of at most 0.011.
The reference program's roundings to bfloat16 on the way count: a program that leaves them out, or rounds other values in their place, can miss the bound.
Values may be sent and summed in bfloat16 or wider, within the bound.
A program may use at most 64 MiB of HBM per device.

```python
import math
import jax
import jax.numpy as jnp
from jax import lax

NLAT = 768
NLON = 1536
NW = 512
TRACERS = 4
STEPS = 1
PLAT = 3
PLON = 256
SWEEPS = 5
OBS = 128
REACTIONS = 12
M = 32
NPY = 256
NPX = 6


def with_ends(array, own_key, low, high):
    longest = array.shape.index(max(array.shape))
    spots = []
    for shift in (0, 1):
        where = [jax.random.randint(jax.random.fold_in(own_key, axis), (), 0, length) for axis, length in enumerate(array.shape)]
        where[longest] = (where[longest] + shift) % array.shape[longest]
        spots.append(tuple(where))
    return array.at[spots[0]].set(low).at[spots[1]].set(high)


def block_scale(own_key, shape, split, smallest, top_value):
    def one(axis_at, parts):
        steps = jax.random.uniform(jax.random.fold_in(jax.random.fold_in(own_key, 6), axis_at), (parts,), jnp.float32, smallest / len(split), top_value / len(split))
        return jnp.repeat(jnp.exp(steps), shape[axis_at] // parts).reshape((-1,) + (1,) * (len(shape) - axis_at - 1))

    loudness = one(*split[0])
    for cut in split[1:]:
        loudness = loudness * one(*cut)
    return loudness


def setup_inputs(seed: int = 0) -> dict:
    key_list = jax.random.split(jax.random.key(seed), 7)
    initial_concentrations = jnp.clip(0.5 + 1.5 * jax.random.uniform(key_list[0], (M, TRACERS, NLAT, NLON), jnp.float32) ** block_scale(key_list[0], (M, TRACERS, NLAT, NLON), ((0, 8), (2, 32)), -0.2, 0.2), 0.5, 2.0)
    rate_field = jnp.clip(jnp.exp(math.log(0.29882812) - 2.7092764 * jax.random.uniform(key_list[1], (REACTIONS, NLAT, NLON), jnp.float32) ** block_scale(key_list[1], (REACTIONS, NLAT, NLON), ((1, 32),), -0.2, 0.2)), 0.019897461, 0.29882812).astype(jnp.bfloat16)
    kinetic_scaling_factors = jnp.clip(jnp.exp(math.log(2.0) - 1.3862944 * jax.random.uniform(key_list[2], (M, REACTIONS, NPY, NPX), jnp.float32) ** block_scale(key_list[2], (M, REACTIONS, NPY, NPX), ((0, 8), (2, 32)), -0.2, 0.2)), 0.5, 2.0).astype(jnp.bfloat16)
    observed_cell = with_ends(jax.random.randint(key_list[3], (NPY, NPX, OBS), 0, TRACERS * PLAT * PLON), jax.random.fold_in(key_list[3], 1), 0, (TRACERS * PLAT * PLON) - 1).astype(jnp.int32)
    measured_value = jnp.clip(0.5 + 1.5 * jax.random.uniform(key_list[4], (NPY, NPX, OBS), jnp.float32) ** block_scale(key_list[4], (NPY, NPX, OBS), ((0, 32),), -0.2, 0.2), 0.5, 2.0)
    error_variance = jnp.clip(jnp.exp(math.log(0.5) - 2.3025851 * jax.random.uniform(key_list[5], (NPY, NPX, OBS), jnp.float32) ** block_scale(key_list[5], (NPY, NPX, OBS), ((0, 32),), -0.2, 0.2)), 0.05, 0.5)
    return dict(initial_concentrations=initial_concentrations, rate_field=rate_field, kinetic_scaling_factors=kinetic_scaling_factors, observed_cell=observed_cell, measured_value=measured_value, error_variance=error_variance)


damping = 2.0

def zonal_lookup(longitudes, wavenumbers):
    column = jnp.arange(longitudes, dtype=jnp.int32)
    wave = jnp.arange(wavenumbers, dtype=jnp.int32)
    phase = wave[:, None] * column[None, :] % longitudes
    angle = phase.astype(jnp.float32) * (2.0 * math.pi / longitudes)
    cosine = jnp.cos(angle)
    sine = jnp.sin(angle)
    forward = jnp.stack([cosine, -sine], axis=1).reshape(2 * wavenumbers, longitudes).T.astype(jnp.bfloat16)
    weight = jnp.where(wave == 0, 1.0, 2.0).astype(jnp.float32)[:, None]
    inverse = jnp.stack([weight * cosine, -weight * sine], axis=1).reshape(2 * wavenumbers, longitudes).astype(jnp.bfloat16)
    return (forward, inverse)

def meridional_table(wave_ids, latitudes, wavenumbers):
    modes = jnp.arange(wavenumbers, dtype=jnp.int32)
    theta = (jnp.arange(latitudes, dtype=jnp.float32) + 0.5) * (math.pi / latitudes)
    order = modes.astype(jnp.float32)
    cosine = jnp.cos(theta[:, None] * order[None, :])
    sine = jnp.sin(theta[:, None] * (order[None, :] + 1.0))
    even = (wave_ids % 2 == 0)[:, None, None]
    kept = (modes[None, :] + wave_ids[:, None] <= wavenumbers - 1)[:, None, :]
    return jnp.where(kept, jnp.where(even, cosine[None], sine[None]), 0.0).astype(jnp.bfloat16)

def spectral_gain(wave_ids, wavenumbers):
    modes = jnp.arange(wavenumbers, dtype=jnp.int32)
    total = (wave_ids[:, None] + modes[None, :]).astype(jnp.float32)
    ratio = total * (total + 1.0) / float(wavenumbers * (wavenumbers - 1))
    half = jnp.where((wave_ids[:, None] % 2 == 0) & (modes[None, :] == 0), 0.5, 1.0)
    return (half / (1.0 + damping * ratio * ratio)).astype(jnp.float32)

def local_rates(factors, photolysis, patch_rows, patch_cols):
    reactions, rows, cols = photolysis.shape
    shaped = photolysis.astype(jnp.float32).reshape(reactions, rows // patch_rows, patch_rows, cols // patch_cols, patch_cols)
    scaled = factors.astype(jnp.float32)[..., :, :, None, :, None] * shaped
    return scaled.reshape(factors.shape[:-2] + (rows, cols))

def react(tracer_amounts, rates):
    count = tracer_amounts.shape[-3]
    others = count - 1
    leave = []
    for source in range(count):
        outflow = rates[..., others * source, :, :]
        for turn in range(1, others):
            outflow = outflow + rates[..., others * source + turn, :, :]
        leave.append(1.0 / (1.0 + outflow))
    result = []
    for target in range(count):
        value = tracer_amounts[..., target, :, :] * leave[target]
        for source in range(count):
            if source != target:
                turn = target if target < source else target - 1
                value = value + rates[..., others * source + turn, :, :] * leave[source] * tracer_amounts[..., source, :, :]
        result.append(value)
    return jnp.stack(result, axis=-3)

def ensemble_update(patches, theta, positions, observed, variance):
    highest = lax.Precision.HIGHEST
    members = patches.shape[1]
    values = patches.astype(jnp.float32)
    midpoint = lax.optimization_barrier(jnp.mean(values, axis=1, keepdims=True))
    perturbation = values - midpoint
    index_full = jnp.broadcast_to(positions[:, None, :], (positions.shape[0], members, positions.shape[1]))
    predicted = jnp.take_along_axis(values, index_full, axis=2)
    seen_mean = lax.optimization_barrier(jnp.mean(predicted, axis=1, keepdims=True))
    seen_spread = predicted - seen_mean
    weighted = seen_spread * (1.0 / variance)[:, None, :]
    outer = jnp.einsum('pik,pjk->pij', weighted, seen_spread, precision=highest)
    scale = members - 1.0 + jnp.sqrt(lax.optimization_barrier(jnp.sum(outer * outer, axis=(1, 2))))
    identity = jnp.eye(members, dtype=jnp.float32)
    current = ((members - 1.0) * identity + outer) / scale[:, None, None]
    root = jnp.broadcast_to(identity, current.shape)
    for sweep in range(SWEEPS):
        middle = 1.5 * identity - 0.5 * jnp.einsum('pij,pjk->pik', root, current, precision=highest)
        current = jnp.einsum('pij,pjk->pik', current, middle, precision=highest)
        root = jnp.einsum('pij,pjk->pik', middle, root, precision=highest)
    covariance = jnp.einsum('pij,pjk->pik', root, root, precision=highest) / scale[:, None, None]
    innovation = observed - seen_mean[:, 0, :]
    projected = jnp.einsum('pjk,pk->pj', weighted, innovation, precision=highest)
    average_coefficient = jnp.einsum('pij,pj->pi', covariance, projected, precision=highest)
    transform = jnp.sqrt((members - 1.0) / scale)[:, None, None] * root + average_coefficient[:, :, None]
    analysis = midpoint + jnp.einsum('pik,pij->pjk', perturbation, transform, precision=highest)
    theta_mean = lax.optimization_barrier(jnp.mean(theta, axis=1, keepdims=True))
    theta_new = theta_mean + jnp.einsum('pir,pij->pjr', theta - theta_mean, transform, precision=highest)
    return (analysis.astype(jnp.bfloat16), jnp.exp(theta_new).astype(jnp.bfloat16))

def reference(initial_concentrations, rate_field, kinetic_scaling_factors, observed_cell, measured_value, error_variance):
    forward, inverse = zonal_lookup(NLON, NW)
    block = min(NW, 64)

    def one_block(bundled_realizations):
        piece, first = bundled_realizations
        wave_ids = first + jnp.arange(block, dtype=jnp.int32)
        table = meridional_table(wave_ids, NLAT, NW).astype(jnp.float32)
        gain = spectral_gain(wave_ids, NW)
        spectrum = jnp.einsum('fjmc,mjk->fmck', piece.astype(jnp.float32), table) * (2.0 / NLAT)
        damped = (spectrum * gain[None, :, None, :]).astype(jnp.bfloat16)
        back = jnp.einsum('fmck,mjk->fjmc', damped.astype(jnp.float32), table)
        return back.astype(jnp.bfloat16)

    def meridional(fourier):
        pieces = fourier.reshape(TRACERS, NLAT, NW // block, block, 2).transpose(2, 0, 1, 3, 4)
        firsts = jnp.arange(NW // block, dtype=jnp.int32) * block
        backs = lax.map(one_block, (pieces, firsts))
        return backs.transpose(1, 2, 0, 3, 4).reshape(TRACERS, NLAT, 2 * NW)

    def predicted_concentration(bundled_realizations):
        tracer_amounts, factors = bundled_realizations
        rates = local_rates(factors, rate_field, PLAT, PLON)
        for step in range(STEPS):
            flat = tracer_amounts.astype(jnp.bfloat16).reshape(TRACERS * NLAT, NLON)
            fourier = (jnp.dot(flat, forward, preferred_element_type=jnp.float32) * (1.0 / NLON)).astype(jnp.bfloat16)
            back = meridional(fourier.reshape(TRACERS, NLAT, NW, 2))
            smooth = jnp.dot(back.reshape(TRACERS * NLAT, 2 * NW), inverse, preferred_element_type=jnp.float32)
            tracer_amounts = react(smooth.reshape(TRACERS, NLAT, NLON), rates)
        return tracer_amounts.astype(jnp.bfloat16)
    background_concentrations = lax.map(predicted_concentration, (initial_concentrations, kinetic_scaling_factors))
    rows_count = NLAT // PLAT
    cols_count = NLON // PLON
    cells = TRACERS * PLAT * PLON
    patches = background_concentrations.reshape(M, TRACERS, rows_count, PLAT, cols_count, PLON).transpose(2, 4, 0, 1, 3, 5).reshape(rows_count, cols_count, M, cells)
    theta = jnp.log(kinetic_scaling_factors.astype(jnp.float32)).transpose(2, 3, 0, 1)

    def one_row(bundled_realizations):
        row_patches, row_theta, row_cells, row_values, line_dispersion = bundled_realizations
        return ensemble_update(row_patches, row_theta, row_cells, row_values, line_dispersion)
    new_rows, new_rates = lax.map(one_row, (patches, theta, observed_cell, measured_value, error_variance))
    analysis = new_rows.reshape(rows_count, cols_count, M, TRACERS, PLAT, PLON).transpose(2, 3, 0, 4, 1, 5).reshape(M, TRACERS, NLAT, NLON)
    mult_analysis = new_rates.transpose(2, 3, 0, 1)
    return (analysis, mult_analysis)
```

```python
import functools
import math

import jax
import jax.numpy as jnp
import ml_dtypes
import numpy as np
from jax import lax
from jax.experimental import pallas as pl
from jax.experimental.pallas import tpu as pltpu
from jax.sharding import PartitionSpec as P

NLAT = 768
NLON = 1536
NW = 512
PLAT = 3
PLON = 256
SWEEPS = 5
TRACERS = 4
MEMBERS = 32
REACTIONS = 12
DAMPING = 2.0

GROUPS = 8
BANDS = 32
LOCAL = 4
BLOCKS = 8
BAND = NLAT // BANDS
PATCHES = NLON // PLON
ROWS = TRACERS * PLAT
MESH = pl.DeviceIdType.MESH
HI = lax.Precision.HIGHEST
ZSTEPS = (4, 3, 5, 2, 6, 1, 7, 0)
PAIRS = ((1, 1), (0, 1), (1, 0), (0, 0))

f32 = jnp.float32
bf16 = jnp.bfloat16


def wave_numbers():
    block = np.arange(BLOCKS)[:, None]
    place = np.arange(NW // BLOCKS)[None, :]
    return 2 * ((block // 2) * (NW // BLOCKS) + place) + block % 2


@functools.lru_cache(maxsize=1)
def tables():
    waves = wave_numbers()
    m = waves.reshape(-1)
    phase = (m[:, None] * np.arange(NLON)[None, :]) % NLON
    angle = phase.astype(np.float32) * np.float32(2.0 * math.pi / NLON)
    cosine, sine = np.cos(angle), np.sin(angle)
    forward = np.stack([cosine, -sine], axis=1).reshape(2 * NW, NLON).T
    forward = forward.reshape(NLON, 4, 256).transpose(1, 0, 2)
    weight = np.where(m == 0, 1.0, 2.0).astype(np.float32)[:, None]
    inverse = np.stack([weight * cosine, -weight * sine], axis=1).reshape(2 * NW, NLON)
    inverse = inverse.reshape(2 * NW, PATCHES, PLON).transpose(1, 0, 2)

    order = np.arange(NW, dtype=np.float32)
    theta = (np.arange(NLAT, dtype=np.float32) + np.float32(0.5)) * np.float32(math.pi / NLAT)
    even = np.cos(theta[:, None] * order[None, :])
    odd = np.sin(theta[:, None] * (order[None, :] + np.float32(1.0)))
    both = np.stack([even, odd])
    to_modes = both.transpose(0, 2, 1)
    dest = np.arange(GROUPS)[:, None, None], np.arange(BANDS)[None, :, None], np.arange(PLAT)
    rows = (dest[1] * BAND + dest[0] * PLAT + dest[2]).reshape(-1)
    to_rows = both[:, rows, :]

    total = (waves[:, None, :] + np.arange(NW)[None, :, None]).astype(np.float32)
    ratio = total * (total + np.float32(1.0)) / np.float32(NW * (NW - 1))
    half = np.where((waves[:, None, :] % 2 == 0) & (np.arange(NW)[None, :, None] == 0), 0.5, 1.0)
    gain = (half / (1.0 + DAMPING * ratio * ratio)).astype(np.float32) * np.float32(2.0 / NLAT)
    gain = np.where(total <= NW - 1, gain, 0.0).astype(np.float32)
    gain = np.repeat(gain, 2, axis=2)

    spread = np.zeros((BANDS, 16, TRACERS, BANDS, PLAT), np.float32)
    for b in range(BANDS):
        for t in range(TRACERS):
            for j in range(PLAT):
                spread[b, t * PLAT + j, t, b, j] = 1.0
    spread = spread.reshape(BANDS * 16, TRACERS * BANDS * PLAT)
    gather = np.zeros((ROWS, MEMBERS, MEMBERS, 16), np.float32)
    for e in range(MEMBERS):
        for a in range(ROWS):
            gather[a, e, e, a] = 1.0
    gather = gather.reshape(ROWS * MEMBERS, MEMBERS * 16)
    home = np.zeros((GROUPS, LOCAL, ROWS, ROWS, GROUPS, LOCAL), np.float32)
    for g in range(GROUPS):
        for e in range(LOCAL):
            for a in range(ROWS):
                home[g, e, a, a, g, e] = 1.0
    home = home.reshape(MEMBERS * ROWS, ROWS * MEMBERS)
    b = lambda v: np.asarray(v, np.float32).astype(ml_dtypes.bfloat16)
    return b(forward), b(inverse), b(to_modes), b(to_rows), gain, b(spread), b(gather), b(home)


def split_grid(b):
    return b // 16, lax.rem(b // 2, 8), lax.rem(b, 2)


def peer(group_step, a, dz, c):
    g, b = lax.axis_index("mem"), lax.axis_index("grid")
    half, z, core = split_grid(b)
    band = lax.rem(half + a, 2) * 16 + lax.rem(z + dz, 8) * 2 + lax.rem(core + c, 2)
    return lax.rem(g + group_step, GROUPS), band


def kernel(
    x_hbm,
    fac,
    cells,
    measured,
    variance,
    field_hbm,
    forward_hbm,
    inverse_hbm,
    modes_hbm,
    rows_hbm,
    gain_hbm,
    spread_hbm,
    gather_hbm,
    home_hbm,
    out_hbm,
    mult_out,
    x,
    xb,
    forward,
    inverse,
    modes,
    rows,
    gain,
    spread,
    gather,
    home,
    field,
    field_rows,
    send1,
    recv1,
    staged,
    plane,
    damped,
    send2,
    recv2,
    padded,
    coefficients,
    fac_in,
    fac_wide,
    background,
    weighted,
    spread_seen,
    projected,
    transform,
    send3,
    mult_send,
    mult_in,
    load_sem,
    local_sem,
    send_sem,
    recv_sem,
):
    g, b = lax.axis_index("mem"), lax.axis_index("grid")
    half, z, core = split_grid(b)
    member = half * 2 + core

    def load(src, dst, i):
        return pltpu.make_async_copy(src, dst, load_sem.at[i])

    load_x = load(x_hbm, x, 0)
    load_x.start()
    load_forward = [load(forward_hbm.at[i], forward.at[i], 1 + i) for i in range(4)]
    for one in load_forward:
        one.start()
    parity = lax.rem(z, 2)
    later = [
        load(modes_hbm.at[parity], modes, 5),
        load(rows_hbm.at[parity], rows, 6),
        load(gain_hbm.at[z], gain, 7),
        load(spread_hbm, spread, 8),
        load(field_hbm, field, 9),
        load(inverse_hbm, inverse, 10),
        load(gather_hbm, gather, 11),
        load(home_hbm, home, 12),
    ]
    for one in later:
        one.start()

    barrier = pltpu.get_barrier_semaphore()

    def greet(step, carry):
        for a, c in PAIRS:
            for dz in ZSTEPS:

                def signal():
                    pl.semaphore_signal(
                        barrier, inc=1, device_id=peer(step, a, dz, c), device_id_type=MESH
                    )

                if a or c or dz:
                    signal()
                else:
                    pl.when(step != 0)(signal)
        return carry

    lax.fori_loop(0, GROUPS, greet, 0)

    load_x.wait()
    xb[...] = x[...].reshape(LOCAL * TRACERS * BAND, NLON).astype(bf16)
    for one in load_forward:
        one.wait()

    def forward_step(i, carry):
        value = jnp.dot(xb[...], forward[i], preferred_element_type=f32) * (1.0 / NLON)
        value = value.astype(bf16).reshape(LOCAL, TRACERS * BAND, 256)
        send1[2 * i] = value[:, :, :128]
        send1[2 * i + 1] = value[:, :, 128:]
        return carry

    lax.fori_loop(0, 4, forward_step, 0)
    pl.semaphore_wait(barrier, GROUPS * BANDS - 1)

    def remote(src, dst, i, to):
        return pltpu.make_async_remote_copy(
            src_ref=src,
            dst_ref=dst,
            send_sem=send_sem.at[i],
            recv_sem=recv_sem.at[i],
            device_id=to,
            device_id_type=MESH,
        )

    def wait_bytes(ref, sem):
        pltpu.make_async_copy(ref, ref, sem).wait()

    for a, c in PAIRS:
        for dz in ZSTEPS:
            if a or c or dz:
                _, band = peer(0, a, dz, c)
                h2, z2, c2 = split_grid(band)
                remote(send1.at[z2, h2 * 2 + c2], recv1.at[b], 0, (g, band)).start()
    own1 = pltpu.make_async_copy(send1.at[z, member], recv1.at[b], local_sem.at[0])
    own1.start()
    for step in range(1, GROUPS):
        to = lax.rem(g + step, GROUPS)
        remote(fac.at[to], fac_in.at[g], 1, (to, b)).start()
    own_fac = pltpu.make_async_copy(fac.at[g], fac_in.at[g], local_sem.at[1])
    own_fac.start()

    for one in later:
        one.wait()
    padded[...] = jnp.zeros(padded.shape, f32)

    line_of = lax.broadcasted_iota(jnp.int32, (8, BAND), 0) + g * PLAT
    own_lines = jnp.where(line_of == lax.broadcasted_iota(jnp.int32, (8, BAND), 1), 1.0, 0.0)
    own_lines = own_lines.astype(bf16)

    def widen(r, carry):
        field_rows[r] = jnp.dot(own_lines, field[r], preferred_element_type=f32)
        return carry

    lax.fori_loop(0, REACTIONS, widen, 0)
    own_fac.wait()
    wait_bytes(fac_in.at[pl.ds(0, GROUPS - 1)], recv_sem.at[1])
    wait_bytes(fac.at[pl.ds(0, GROUPS - 1)], send_sem.at[1])
    row_of = lax.broadcasted_iota(jnp.int32, (MEMBERS, GROUPS * 8), 0)
    col_of = lax.broadcasted_iota(jnp.int32, (MEMBERS, GROUPS * 8), 1)
    pick = jnp.where(col_of == (row_of // LOCAL) * 8 + lax.rem(row_of, LOCAL), 1.0, 0.0)
    factors = jnp.dot(
        pick.astype(bf16),
        fac_in[...].reshape(GROUPS * 8, 128).astype(bf16),
        preferred_element_type=f32,
    )
    for c in range(PATCHES):
        for r in range(REACTIONS):
            lane = c * REACTIONS + r
            fac_wide[c, r] = jnp.broadcast_to(factors[:, lane : lane + 1], (MEMBERS, 128))
    log_rate = jnp.log(factors)
    log_mean = jnp.mean(log_rate, axis=0, keepdims=True)
    log_spread = log_rate - log_mean

    own1.wait()
    wait_bytes(recv1.at[pl.ds(0, BANDS - 1)], recv_sem.at[0])

    def unpack(s, carry):
        value = recv1[s].astype(f32)
        at = pl.ds(pl.multiple_of(s * BAND, 8), BAND)
        for t in range(TRACERS):
            staged[at, t * 128 : (t + 1) * 128] = value[t * BAND : (t + 1) * BAND]
        return carry

    lax.fori_loop(0, BANDS, unpack, 0)
    plane[...] = staged[...].astype(bf16)

    def to_modes(i, carry):
        at = pl.ds(pl.multiple_of(i * 128, 128), 128)
        value = jnp.dot(modes[at, :], plane[...], preferred_element_type=f32)
        scale = gain[at, :]
        for t in range(TRACERS):
            lanes = slice(t * 128, (t + 1) * 128)
            damped[at, lanes] = (value[:, lanes] * scale).astype(bf16)
        return carry

    lax.fori_loop(0, NW // 128, to_modes, 0)

    def to_owner(step, carry):
        owner = lax.rem(g + step, GROUPS)
        at = pl.ds(pl.multiple_of(owner * 96, 32), 96)
        value = jnp.dot(rows[at, :], damped[...], preferred_element_type=f32).astype(bf16)
        stacked = jnp.concatenate([value[:, t * 128 : (t + 1) * 128] for t in range(TRACERS)], 0)
        wide = jnp.dot(spread[...], stacked, preferred_element_type=f32)
        wide = wide.reshape(BANDS, 16, 128).astype(bf16)
        send2[pl.ds(owner * BANDS, BANDS)] = wide[:, :ROWS]
        for a, c in PAIRS:
            for dz in ZSTEPS:
                to = peer(step, a, dz, c)

                def push():
                    remote(
                        send2.at[owner * BANDS + to[1]],
                        recv2.at[g, half, z, core],
                        2,
                        (owner, to[1]),
                    ).start()

                if a or c or dz:
                    push()
                else:
                    pl.when(step != 0)(push)
        return carry

    lax.fori_loop(0, GROUPS, to_owner, 0)
    own2 = pltpu.make_async_copy(
        send2.at[g * BANDS + b], recv2.at[g, half, z, core], local_sem.at[2]
    )
    own2.start()
    own2.wait()
    wait_bytes(send2.at[pl.ds(0, GROUPS * BANDS - 1)], recv_sem.at[2])

    for block in range(BLOCKS):
        value = recv2[:, :, block, :, :, :].astype(f32).reshape(MEMBERS, ROWS, 128)
        padded[:, :ROWS, block * 128 : (block + 1) * 128] = value

    def permute(i, carry):
        lanes = pl.ds(pl.multiple_of(i * 256, 256), 256)
        value = padded[:, :, lanes].reshape(MEMBERS * 16, 256).astype(bf16)
        coefficients[:, lanes] = jnp.dot(
            gather[...], value, preferred_element_type=f32
        ).astype(bf16)
        return carry

    lax.fori_loop(0, 4, permute, 0)

    obs = cells.shape[-1]

    def background_step(c, carry):
        smooth = jnp.dot(coefficients[...], inverse[c], preferred_element_type=f32)
        smooth = smooth.reshape(TRACERS, PLAT, MEMBERS, PLON)
        for j in range(PLAT):
            for h in range(PLON // 128):
                lanes = pl.ds(pl.multiple_of(c * PLON + h * 128, 128), 128)
                tracers = [smooth[t, j, :, h * 128 : (h + 1) * 128] for t in range(TRACERS)]
                rates = []
                for r in range(REACTIONS):
                    line = field_rows[r, j : j + 1, lanes]
                    rates.append(fac_wide[c, r] * line)
                leave, gone = [], []
                for s in range(TRACERS):
                    outflow = rates[3 * s] + rates[3 * s + 1] + rates[3 * s + 2]
                    leave.append(1.0 / (1.0 + outflow))
                    gone.append(leave[s] * tracers[s])
                for t in range(TRACERS):
                    value = gone[t]
                    for s in range(TRACERS):
                        if s != t:
                            value = value + rates[3 * s + (t if t < s else t - 1)] * gone[s]
                    row = (t * PLAT + j) * MEMBERS
                    background[c, row : row + MEMBERS, h * 128 : (h + 1) * 128] = value.astype(
                        bf16
                    )
        cell = cells[g, pl.ds(c, 1), :]
        column = jnp.bitwise_and(cell, PLON - 1)
        row = lax.shift_right_logical(cell, 8)
        picker = jnp.where(
            lax.broadcasted_iota(jnp.int32, (PLON, obs), 0) == column, 1.0, 0.0
        ).astype(bf16)
        seen = jnp.dot(background[c], picker, preferred_element_type=f32)
        predicted = jnp.zeros((MEMBERS, obs), f32)
        for k in range(ROWS):
            predicted = predicted + jnp.where(
                row == k, seen[k * MEMBERS : (k + 1) * MEMBERS], 0.0
            )
        seen_mean = jnp.mean(predicted, axis=0, keepdims=True)
        spread_of = predicted - seen_mean
        weight = spread_of * (1.0 / variance[g, pl.ds(c, 1), :])
        innovation = measured[g, pl.ds(c, 1), :] - seen_mean
        at = pl.ds(pl.multiple_of(c * MEMBERS, MEMBERS), MEMBERS)
        weighted[at, :] = weight
        spread_seen[at, :] = spread_of
        projected[at, :] = jnp.broadcast_to(
            jnp.sum(weight * innovation, axis=1, keepdims=True), (MEMBERS, 128)
        )
        return carry

    lax.fori_loop(0, PATCHES, background_step, 0)

    size = PATCHES * MEMBERS
    block_row = lax.broadcasted_iota(jnp.int32, (size, size), 0)
    block_col = lax.broadcasted_iota(jnp.int32, (size, size), 1)
    same = block_row // MEMBERS == block_col // MEMBERS
    identity = jnp.where(block_row == block_col, 1.0, 0.0)

    def exact(left, right):
        return jnp.dot(left, right, precision=HI, preferred_element_type=f32)

    outer = lax.dot_general(
        weighted[...],
        spread_seen[...],
        (((1,), (1,)), ((), ())),
        precision=HI,
        preferred_element_type=f32,
    )
    outer = jnp.where(same, outer, 0.0)
    square = jnp.sum(outer * outer, axis=1, keepdims=True).reshape(PATCHES, MEMBERS, 1)
    square = jnp.broadcast_to(jnp.sum(square, axis=1, keepdims=True), (PATCHES, MEMBERS, 1))
    scale = (MEMBERS - 1.0) + jnp.sqrt(square.reshape(size, 1))
    current = ((MEMBERS - 1.0) * identity + outer) / scale
    root = 1.5 * identity - 0.5 * current
    current = exact(current, root)
    for sweep in range(1, SWEEPS):
        middle = 1.5 * identity - 0.5 * exact(root, current)
        if sweep < SWEEPS - 1:
            current = exact(current, middle)
        root = exact(middle, root)
    mean_weight = exact(root, exact(root, projected[...])) / scale
    full = jnp.where(same, jnp.sqrt((MEMBERS - 1.0) / scale) * root, 0.0)
    fold = jnp.where(
        lax.rem(lax.broadcasted_iota(jnp.int32, (size, MEMBERS), 0), MEMBERS)
        == lax.broadcasted_iota(jnp.int32, (size, MEMBERS), 1),
        1.0,
        0.0,
    )
    transform[...] = exact(full, fold) + mean_weight[:, :MEMBERS]

    def apply(matrix, values, precision=None):
        return lax.dot_general(
            matrix,
            values,
            (((0,), (0,)), ((), ())),
            precision=precision,
            preferred_element_type=f32,
        )

    def analysis_step(c, carry):
        matrix = transform[pl.ds(pl.multiple_of(c * MEMBERS, MEMBERS), MEMBERS), :]
        pieces = []
        for k in range(ROWS):
            value = background[c, k * MEMBERS : (k + 1) * MEMBERS, :].astype(f32)
            center = jnp.mean(value, axis=0, keepdims=True)
            pieces.append((center + apply(matrix, value - center)).astype(bf16))
        analysed = jnp.concatenate(pieces, axis=0)
        sent = jnp.dot(home[...], analysed, preferred_element_type=f32).astype(bf16)
        send3[c] = sent.reshape(GROUPS, LOCAL * ROWS, PLON)
        lanes = pl.ds(pl.multiple_of(c * PLON, PLON), PLON)
        for step in range(1, GROUPS):
            to = lax.rem(g + step, GROUPS)
            remote(send3.at[c, to], out_hbm.at[g, :, lanes], 3, (to, b)).start()
        pltpu.make_async_copy(
            send3.at[c, g], out_hbm.at[g, :, lanes], local_sem.at[3]
        ).start()
        lane = lax.broadcasted_iota(jnp.int32, (MEMBERS, 128), 1)
        mine = jnp.logical_and(lane >= c * REACTIONS, lane < (c + 1) * REACTIONS)
        return carry + jnp.where(mine, apply(matrix, log_spread, HI), 0.0)

    change = lax.fori_loop(0, PATCHES, analysis_step, jnp.zeros((MEMBERS, 128), f32))
    mult = jnp.exp(log_mean + change).astype(bf16)
    back_row = lax.broadcasted_iota(jnp.int32, (GROUPS * 8, MEMBERS), 0)
    back_col = lax.broadcasted_iota(jnp.int32, (GROUPS * 8, MEMBERS), 1)
    place = (back_col // LOCAL) * 8 + lax.rem(back_col, LOCAL)
    put = jnp.where(back_row == place, 1.0, 0.0).astype(bf16)
    mult_send[...] = jnp.dot(put, mult, preferred_element_type=f32).reshape(GROUPS, 8, 128)
    for step in range(1, GROUPS):
        to = lax.rem(g + step, GROUPS)
        remote(mult_send.at[to], mult_in.at[g], 4, (to, b)).start()
    own_mult = pltpu.make_async_copy(mult_send.at[g], mult_in.at[g], local_sem.at[4])
    own_mult.start()

    own_mult.wait()
    wait_bytes(mult_in.at[pl.ds(0, GROUPS - 1)], recv_sem.at[4])
    mult_out[...] = mult_in[...]
    wait_bytes(send3.at[:, 0], local_sem.at[3])
    wait_bytes(send3.at[:, pl.ds(0, GROUPS - 1)], recv_sem.at[3])
    wait_bytes(send1.at[pl.ds(0, BLOCKS - 1)], send_sem.at[0])
    wait_bytes(send1.at[0, pl.ds(0, LOCAL - 1)], send_sem.at[0])
    wait_bytes(send2.at[pl.ds(0, GROUPS * BANDS - 1)], send_sem.at[2])
    wait_bytes(send3.at[:, pl.ds(0, GROUPS - 1)], send_sem.at[3])
    wait_bytes(mult_send.at[pl.ds(0, GROUPS - 1)], send_sem.at[4])


def on_device(x, field, kinetic, cells, measured, variance):
    forward, inverse, modes, rows, gain, spread, gather, home = tables()
    fac = kinetic.transpose(2, 0, 3, 1).reshape(GROUPS, LOCAL, PATCHES * REACTIONS).astype(f32)
    fac = jnp.pad(
        fac, ((0, 0), (0, 8 - LOCAL), (0, 128 - PATCHES * REACTIONS)), constant_values=1.0
    )
    anywhere = pl.BlockSpec(memory_space=pl.ANY)
    vmem = pl.BlockSpec(memory_space=pltpu.VMEM)
    size = PATCHES * MEMBERS
    scratch = [
        pltpu.VMEM((LOCAL, TRACERS, BAND, NLON), f32),
        pltpu.VMEM((LOCAL * TRACERS * BAND, NLON), bf16),
        pltpu.VMEM((4, NLON, 256), bf16),
        pltpu.VMEM((PATCHES, 2 * NW, PLON), bf16),
        pltpu.VMEM((NW, NLAT), bf16),
        pltpu.VMEM((NLAT, NW), bf16),
        pltpu.VMEM((NW, 128), f32),
        pltpu.VMEM(spread.shape, bf16),
        pltpu.VMEM(gather.shape, bf16),
        pltpu.VMEM(home.shape, bf16),
        pltpu.VMEM((REACTIONS, BAND, NLON), bf16),
        pltpu.VMEM((REACTIONS, 8, NLON), f32),
        pltpu.VMEM((BLOCKS, LOCAL, TRACERS * BAND, 128), bf16),
        pltpu.VMEM((BANDS, TRACERS * BAND, 128), bf16),
        pltpu.VMEM((NLAT, TRACERS * 128), f32),
        pltpu.VMEM((NLAT, TRACERS * 128), bf16),
        pltpu.VMEM((NW, TRACERS * 128), bf16),
        pltpu.VMEM((GROUPS * BANDS, ROWS, 128), bf16),
        pltpu.VMEM((GROUPS, 2, BLOCKS, 2, ROWS, 128), bf16),
        pltpu.VMEM((MEMBERS, 16, BLOCKS * 128), f32),
        pltpu.VMEM((ROWS * MEMBERS, 2 * NW), bf16),
        pltpu.VMEM((GROUPS, 8, 128), f32),
        pltpu.VMEM((PATCHES, REACTIONS, MEMBERS, 128), f32),
        pltpu.VMEM((PATCHES, ROWS * MEMBERS, PLON), bf16),
        pltpu.VMEM((size, 128), f32),
        pltpu.VMEM((size, 128), f32),
        pltpu.VMEM((size, 128), f32),
        pltpu.VMEM((size, MEMBERS), f32),
        pltpu.VMEM((PATCHES, GROUPS, LOCAL * ROWS, PLON), bf16),
        pltpu.VMEM((GROUPS, 8, 128), f32),
        pltpu.VMEM((GROUPS, 8, 128), f32),
        pltpu.SemaphoreType.DMA((13,)),
        pltpu.SemaphoreType.DMA((5,)),
        pltpu.SemaphoreType.DMA((5,)),
        pltpu.SemaphoreType.DMA((5,)),
    ]
    out, mult = pl.pallas_call(
        kernel,
        out_shape=(
            jax.ShapeDtypeStruct((GROUPS, LOCAL * ROWS, NLON), bf16),
            jax.ShapeDtypeStruct((GROUPS, 8, 128), f32),
        ),
        in_specs=[anywhere, vmem, vmem, vmem, vmem, anywhere] + [anywhere] * 8,
        out_specs=(anywhere, vmem),
        scratch_shapes=scratch,
        compiler_params=pltpu.CompilerParams(
            collective_id=0, has_side_effects=True, vmem_limit_bytes=60 << 20
        ),
        name="assimilate",
    )(x, fac, cells, measured, variance, field, forward, inverse, modes, rows, gain, spread, gather, home)
    analysis = (
        out.reshape(GROUPS, LOCAL, TRACERS, PLAT, NLON)
        .transpose(1, 2, 0, 3, 4)
        .reshape(LOCAL, TRACERS, BAND, NLON)
    )
    mult = (
        mult[:, :LOCAL, : PATCHES * REACTIONS]
        .reshape(GROUPS, LOCAL, PATCHES, REACTIONS)
        .transpose(1, 3, 0, 2)
        .astype(bf16)
    )
    return analysis, mult


def solution(mesh):
    return jax.shard_map(
        on_device,
        mesh=mesh,
        in_specs=(
            P("mem", None, "grid", None),
            P(None, "grid", None),
            P("mem", None, "grid", None),
            P("grid", None, None),
            P("grid", None, None),
            P("grid", None, None),
        ),
        out_specs=(P("mem", None, "grid", None), P("mem", None, "grid", None)),
        check_vma=False,
    )
```

```python
import functools
import math

import jax
import jax.numpy as jnp
import ml_dtypes
import numpy as np
from jax import lax
from jax.experimental import pallas as pl
from jax.experimental.pallas import tpu as pltpu
from jax.sharding import PartitionSpec as P

NLAT = 768
NLON = 1536
NW = 512
PLAT = 3
PLON = 256
SWEEPS = 5
TRACERS = 4
MEMBERS = 32
REACTIONS = 12
DAMPING = 2.0

GROUPS = 8
BANDS = 32
LOCAL = 4
BLOCKS = 8
TOGETHER = 3
BAND = NLAT // BANDS
PATCHES = NLON // PLON
ROWS = TRACERS * PLAT
MESH = pl.DeviceIdType.MESH
HI = lax.Precision.HIGHEST

PAIRS = ((1, 1), (0, 1), (1, 0), (0, 0))
ZSTEPS = (4, 3, 5, 2, 6, 1, 7, 0)

f32 = jnp.float32
bf16 = jnp.bfloat16


def wave_numbers():
    block = np.arange(BLOCKS)[:, None]
    place = np.arange(NW // BLOCKS)[None, :]
    return 2 * ((block // 2) * (NW // BLOCKS) + place) + block % 2


@functools.lru_cache(maxsize=1)
def tables():
    waves = wave_numbers()
    m = waves.reshape(-1)
    phase = (m[:, None] * np.arange(NLON)[None, :]) % NLON
    angle = phase.astype(np.float32) * np.float32(2.0 * math.pi / NLON)
    cosine, sine = np.cos(angle), np.sin(angle)
    forward = np.stack([cosine, -sine], axis=1).reshape(2 * NW, NLON).T
    forward = forward.reshape(NLON, 4, 256).transpose(1, 0, 2)
    weight = np.where(m == 0, 1.0, 2.0).astype(np.float32)[:, None]
    inverse = np.stack([weight * cosine, -weight * sine], axis=1).reshape(2 * NW, NLON)
    inverse = inverse.reshape(2 * NW, PATCHES, PLON).transpose(1, 0, 2)

    order = np.arange(NW, dtype=np.float32)
    theta = (np.arange(NLAT, dtype=np.float32) + np.float32(0.5)) * np.float32(math.pi / NLAT)
    even = np.cos(theta[:, None] * order[None, :])
    odd = np.sin(theta[:, None] * (order[None, :] + np.float32(1.0)))
    both = np.stack([even, odd])
    to_modes = both.transpose(0, 2, 1)
    dest = np.arange(GROUPS)[:, None, None], np.arange(BANDS)[None, :, None], np.arange(PLAT)
    rows = (dest[1] * BAND + dest[0] * PLAT + dest[2]).reshape(-1)
    to_rows = both[:, rows, :]

    total = (waves[:, None, :] + np.arange(NW)[None, :, None]).astype(np.float32)
    ratio = total * (total + np.float32(1.0)) / np.float32(NW * (NW - 1))
    half = np.where((waves[:, None, :] % 2 == 0) & (np.arange(NW)[None, :, None] == 0), 0.5, 1.0)
    gain = (half / (1.0 + DAMPING * ratio * ratio)).astype(np.float32) * np.float32(2.0 / NLAT)
    gain = np.where(total <= NW - 1, gain, 0.0).astype(np.float32)
    gain = np.repeat(gain, 2, axis=2)

    spread = np.zeros((BANDS, 16, TRACERS, BANDS, PLAT), np.float32)
    for b in range(BANDS):
        for t in range(TRACERS):
            for j in range(PLAT):
                spread[b, t * PLAT + j, t, b, j] = 1.0
    spread = spread.reshape(BANDS * 16, TRACERS * BANDS * PLAT)
    gather = np.zeros((ROWS, MEMBERS, MEMBERS, 16), np.float32)
    for e in range(MEMBERS):
        for a in range(ROWS):
            gather[a, e, e, a] = 1.0
    gather = gather.reshape(ROWS * MEMBERS, MEMBERS * 16)
    home = np.zeros((GROUPS, LOCAL, ROWS, ROWS, GROUPS, LOCAL), np.float32)
    for g in range(GROUPS):
        for e in range(LOCAL):
            for a in range(ROWS):
                home[g, e, a, a, g, e] = 1.0
    home = home.reshape(MEMBERS * ROWS, ROWS * MEMBERS)
    index = np.arange(LOCAL * PATCHES * GROUPS)
    e, c, g = np.unravel_index(index, (LOCAL, PATCHES, GROUPS))
    by_group = np.zeros((index.size, index.size), np.float32)
    by_group[(g * LOCAL + e) * PATCHES + c, index] = 1.0
    g, e, c = np.unravel_index(index, (GROUPS, LOCAL, PATCHES))
    by_patch = np.zeros((index.size, index.size), np.float32)
    by_patch[(c * GROUPS + g) * LOCAL + e, index] = 1.0
    small = np.stack([by_group, by_patch, by_patch.T, by_group.T])
    index = np.arange(GROUPS * LOCAL * ROWS)
    g, et, j = np.unravel_index(index, (GROUPS, LOCAL * TRACERS, PLAT))
    final = np.zeros((index.size, index.size), np.float32)
    final[(et * GROUPS + g) * PLAT + j, index] = 1.0
    b = lambda v: np.asarray(v, np.float32).astype(ml_dtypes.bfloat16)
    return (
        (b(forward), b(inverse), b(to_modes), b(to_rows), gain)
        + (b(spread), b(gather), b(home), b(small)),
        b(final),
    )


def split_grid(b):
    return b // 16, lax.rem(b // 2, 8), lax.rem(b, 2)


def wrap(value, size):
    return jnp.where(value >= size, value - size, value)


def kernel(
    x_hbm,
    field_hbm,
    fac_hbm,
    cells_hbm,
    measured_hbm,
    variance_hbm,
    forward_hbm,
    inverse_hbm,
    modes_hbm,
    rows_hbm,
    gain_hbm,
    spread_hbm,
    gather_hbm,
    home_hbm,
    small_hbm,
    out_hbm,
    mult_out,
    x,
    xb,
    forward,
    inverse,
    modes,
    rows,
    gain,
    spread,
    gather,
    home,
    small,
    fac_raw,
    cells,
    measured,
    variance,
    field,
    field_rows,
    send1,
    recv1,
    staged,
    plane,
    damped,
    send2,
    recv2,
    padded,
    coefficients,
    fac,
    fac_in,
    fac_wide,
    log_mean,
    log_spread,
    log_new,
    background,
    weighted,
    spread_seen,
    projected,
    transform,
    send3,
    mult_send,
    mult_in,
    load_sem,
    local_sem,
    send_sem,
    recv_sem,
    ready,
):
    g, b = lax.axis_index("mem"), lax.axis_index("grid")
    half, z, core = split_grid(b)
    member = half * 2 + core

    def load(src, dst, i):
        return pltpu.make_async_copy(src, dst, load_sem.at[i])

    load_x = load(x_hbm, x, 0)
    load_x.start()
    load_fac = [load(fac_hbm, fac_raw, 13), load(small_hbm, small, 14)]
    for one in load_fac:
        one.start()
    load_forward = [load(forward_hbm.at[i], forward.at[i], 1 + i) for i in range(4)]
    for one in load_forward:
        one.start()
    parity = lax.rem(z, 2)
    later = [
        load(modes_hbm.at[parity], modes, 5),
        load(rows_hbm.at[parity], rows, 6),
        load(gain_hbm.at[z], gain, 7),
        load(spread_hbm, spread, 8),
        load(field_hbm, field, 9),
        load(inverse_hbm, inverse, 10),
        load(gather_hbm, gather, 11),
        load(home_hbm, home, 12),
        load(cells_hbm, cells, 15),
        load(measured_hbm, measured, 16),
        load(variance_hbm, variance, 17),
    ]
    for one in later:
        one.start()

    barrier = pltpu.get_barrier_semaphore()

    groups = [wrap(g + step, GROUPS) for step in range(1, GROUPS)]
    bands = [
        wrap(half + a, 2) * 16 + wrap(z + dz, BLOCKS) * 2 + wrap(core + c, 2)
        for a, c in PAIRS
        for dz in ZSTEPS
        if a or c or dz
    ]
    for to in groups:
        pl.semaphore_signal(barrier, inc=1, device_id=(to, b), device_id_type=MESH)
    for to in bands:
        pl.semaphore_signal(barrier, inc=1, device_id=(g, to), device_id_type=MESH)

    load_x.wait()
    xb[...] = x[...].reshape(LOCAL * TRACERS * BAND, NLON).astype(bf16)
    for one in load_forward:
        one.wait()

    def forward_step(i, carry):
        value = jnp.dot(xb[...], forward[i], preferred_element_type=f32) * (1.0 / NLON)
        value = value.astype(bf16).reshape(LOCAL, TRACERS * BAND, 256)
        send1[2 * i] = value[:, :, :128]
        send1[2 * i + 1] = value[:, :, 128:]
        return carry

    lax.fori_loop(0, 4, forward_step, 0)
    pl.semaphore_wait(barrier, GROUPS + BANDS - 2)
    for to in groups:
        pl.semaphore_signal(ready, inc=1, device_id=(to, b), device_id_type=MESH)

    def remote(src, dst, i, to):
        return pltpu.make_async_remote_copy(
            src_ref=src,
            dst_ref=dst,
            send_sem=send_sem.at[i],
            recv_sem=recv_sem.at[i],
            device_id=to,
            device_id_type=MESH,
        )

    def wait_bytes(ref, sem):
        pltpu.make_async_copy(ref, ref, sem).wait()

    for band in bands:
        h2, z2, c2 = split_grid(band)
        remote(send1.at[z2, h2 * 2 + c2], recv1.at[b], 0, (g, band)).start()
    own1 = pltpu.make_async_copy(send1.at[z, member], recv1.at[b], local_sem.at[0])
    own1.start()
    pairs = LOCAL * PATCHES
    for one in load_fac:
        one.wait()
    raw = fac_raw[...].astype(f32).reshape(pairs * GROUPS, REACTIONS).astype(bf16)
    fac[...] = jnp.ones(fac.shape, f32)
    raw = jnp.dot(small[0], raw, preferred_element_type=f32)
    fac[:, :, :REACTIONS] = raw.reshape(GROUPS, pairs, REACTIONS)
    for to in groups:
        remote(fac.at[to], fac_in.at[g], 1, (to, b)).start()
    own_fac = pltpu.make_async_copy(fac.at[g], fac_in.at[g], local_sem.at[1])
    own_fac.start()

    for one in later:
        one.wait()
    padded[...] = jnp.zeros(padded.shape, f32)

    line_of = lax.broadcasted_iota(jnp.int32, (8, BAND), 0) + g * PLAT
    own_lines = jnp.where(line_of == lax.broadcasted_iota(jnp.int32, (8, BAND), 1), 1.0, 0.0)
    own_lines = own_lines.astype(bf16)

    def widen(r, carry):
        field_rows[r] = jnp.dot(own_lines, field[r], preferred_element_type=f32)
        return carry

    lax.fori_loop(0, REACTIONS, widen, 0)
    own_fac.wait()
    wait_bytes(fac_in.at[pl.ds(0, GROUPS - 1)], recv_sem.at[1])
    wait_bytes(fac.at[pl.ds(0, GROUPS - 1)], send_sem.at[1])
    factors = jnp.dot(
        small[1],
        fac_in[...].reshape(GROUPS * pairs, 128).astype(bf16),
        preferred_element_type=f32,
    )
    for c in range(PATCHES):
        for r in range(REACTIONS):
            column = factors[c * MEMBERS : (c + 1) * MEMBERS, r : r + 1]
            fac_wide[c, r] = jnp.broadcast_to(column, (MEMBERS, 128))
    log_rate = jnp.log(factors).reshape(PATCHES, MEMBERS, 128)
    log_mean[...] = jnp.broadcast_to(
        jnp.mean(log_rate, axis=1, keepdims=True), (PATCHES, MEMBERS, 128)
    )
    log_spread[...] = log_rate - log_mean[...]

    own1.wait()
    wait_bytes(recv1.at[pl.ds(0, BANDS - 1)], recv_sem.at[0])

    def unpack(s, carry):
        value = recv1[s].astype(f32)
        at = pl.ds(pl.multiple_of(s * BAND, 8), BAND)
        for t in range(TRACERS):
            staged[at, t * 128 : (t + 1) * 128] = value[t * BAND : (t + 1) * BAND]
        return carry

    lax.fori_loop(0, BANDS, unpack, 0)
    plane[...] = staged[...].astype(bf16)

    def to_modes(i, carry):
        at = pl.ds(pl.multiple_of(i * 128, 128), 128)
        value = jnp.dot(modes[at, :], plane[...], preferred_element_type=f32)
        scale = gain[at, :]
        for t in range(TRACERS):
            lanes = slice(t * 128, (t + 1) * 128)
            damped[at, lanes] = (value[:, lanes] * scale).astype(bf16)
        return carry

    lax.fori_loop(0, NW // 128, to_modes, 0)

    def to_owner(step, carry):
        owner = wrap(g + step, GROUPS)
        at = pl.ds(pl.multiple_of(owner * 96, 32), 96)
        value = jnp.dot(rows[at, :], damped[...], preferred_element_type=f32).astype(bf16)
        stacked = jnp.concatenate([value[:, t * 128 : (t + 1) * 128] for t in range(TRACERS)], 0)
        wide = jnp.dot(spread[...], stacked, preferred_element_type=f32)
        wide = wide.reshape(BANDS, 16, 128).astype(bf16)
        send2[pl.ds(owner * BANDS, BANDS)] = wide[:, :ROWS]
        for band in bands:
            remote(
                send2.at[owner * BANDS + band],
                recv2.at[g, half, z, core],
                2,
                (owner, band),
            ).start()

        @pl.when(step != 0)
        def _():
            remote(
                send2.at[owner * BANDS + b], recv2.at[g, half, z, core], 2, (owner, b)
            ).start()

        return carry

    pl.semaphore_wait(ready, GROUPS - 1)
    lax.fori_loop(0, GROUPS, to_owner, 0)
    own2 = pltpu.make_async_copy(
        send2.at[g * BANDS + b], recv2.at[g, half, z, core], local_sem.at[2]
    )
    own2.start()
    own2.wait()
    wait_bytes(send2.at[pl.ds(0, GROUPS * BANDS - 1)], recv_sem.at[2])

    for block in range(BLOCKS):
        value = recv2[:, :, block, :, :, :].astype(f32).reshape(MEMBERS, ROWS, 128)
        padded[:, :ROWS, block * 128 : (block + 1) * 128] = value

    def permute(i, carry):
        lanes = pl.ds(pl.multiple_of(i * 256, 256), 256)
        value = padded[:, :, lanes].reshape(MEMBERS * 16, 256).astype(bf16)
        coefficients[:, lanes] = jnp.dot(
            gather[...], value, preferred_element_type=f32
        ).astype(bf16)
        return carry

    lax.fori_loop(0, 4, permute, 0)

    obs = cells.shape[-1]

    def background_step(i, first):
        c = first + i
        smooth = jnp.dot(coefficients[...], inverse[c], preferred_element_type=f32)
        smooth = smooth.reshape(TRACERS, PLAT, MEMBERS, PLON)
        for j in range(PLAT):
            for h in range(PLON // 128):
                lanes = pl.ds(pl.multiple_of(c * PLON + h * 128, 128), 128)
                tracers = [smooth[t, j, :, h * 128 : (h + 1) * 128] for t in range(TRACERS)]
                rates = []
                for r in range(REACTIONS):
                    line = field_rows[r, j : j + 1, lanes]
                    rates.append(fac_wide[c, r] * line)
                leave, gone = [], []
                for s in range(TRACERS):
                    outflow = rates[3 * s] + rates[3 * s + 1] + rates[3 * s + 2]
                    leave.append(1.0 / (1.0 + outflow))
                    gone.append(leave[s] * tracers[s])
                for t in range(TRACERS):
                    value = gone[t]
                    for s in range(TRACERS):
                        if s != t:
                            value = value + rates[3 * s + (t if t < s else t - 1)] * gone[s]
                    row = (t * PLAT + j) * MEMBERS
                    background[c, row : row + MEMBERS, h * 128 : (h + 1) * 128] = value.astype(
                        bf16
                    )
        cell = cells[c, pl.ds(g, 1), :]
        column = jnp.bitwise_and(cell, PLON - 1)
        row = lax.shift_right_logical(cell, 8)
        picker = jnp.where(
            lax.broadcasted_iota(jnp.int32, (PLON, obs), 0) == column, 1.0, 0.0
        ).astype(bf16)
        seen = jnp.dot(background[c], picker, preferred_element_type=f32)
        predicted = jnp.zeros((MEMBERS, obs), f32)
        for k in range(ROWS):
            predicted = predicted + jnp.where(
                row == k, seen[k * MEMBERS : (k + 1) * MEMBERS], 0.0
            )
        seen_mean = jnp.mean(predicted, axis=0, keepdims=True)
        spread_of = predicted - seen_mean
        weight = spread_of * (1.0 / variance[c, pl.ds(g, 1), :])
        innovation = measured[c, pl.ds(g, 1), :] - seen_mean
        at = pl.ds(pl.multiple_of(i * MEMBERS, MEMBERS), MEMBERS)
        weighted[at, :] = weight
        spread_seen[at, :] = spread_of
        projected[at, :] = jnp.broadcast_to(
            jnp.sum(weight * innovation, axis=1, keepdims=True), (MEMBERS, 128)
        )
        return first

    size = TOGETHER * MEMBERS
    block_row = lax.broadcasted_iota(jnp.int32, (size, size), 0)
    block_col = lax.broadcasted_iota(jnp.int32, (size, size), 1)
    same = block_row // MEMBERS == block_col // MEMBERS
    identity = jnp.where(block_row == block_col, 1.0, 0.0)

    def halves(value):
        high = value.astype(bf16)
        return high, (value - high.astype(f32)).astype(bf16)

    def exact(left, right):
        (a, b), (c, d) = halves(left), halves(right)
        dot = functools.partial(jnp.dot, preferred_element_type=f32)
        return dot(a, c) + (dot(a, d) + dot(b, c))

    def solve():
        outer = lax.dot_general(
            weighted[...],
            spread_seen[...],
            (((1,), (1,)), ((), ())),
            precision=HI,
            preferred_element_type=f32,
        )
        outer = jnp.where(same, outer, 0.0)
        square = jnp.sum(outer * outer, axis=1, keepdims=True).reshape(TOGETHER, MEMBERS, 1)
        square = jnp.broadcast_to(jnp.sum(square, axis=1, keepdims=True), (TOGETHER, MEMBERS, 1))
        scale = (MEMBERS - 1.0) + jnp.sqrt(square.reshape(size, 1))
        current = ((MEMBERS - 1.0) * identity + outer) / scale
        root = 1.5 * identity - 0.5 * current
        current = exact(current, root)
        for sweep in range(1, SWEEPS):
            middle = 1.5 * identity - 0.5 * exact(root, current)
            if sweep < SWEEPS - 1:
                current = exact(current, middle)
            root = exact(middle, root)
        mean_weight = exact(root, exact(root, projected[...])) / scale
        full = jnp.where(same, jnp.sqrt((MEMBERS - 1.0) / scale) * root, 0.0)
        fold = jnp.where(
            lax.rem(lax.broadcasted_iota(jnp.int32, (size, MEMBERS), 0), MEMBERS)
            == lax.broadcasted_iota(jnp.int32, (size, MEMBERS), 1),
            1.0,
            0.0,
        )
        transform[...] = exact(full, fold) + mean_weight[:, :MEMBERS]

    def apply(matrix, values, precision=None):
        return lax.dot_general(
            matrix,
            values,
            (((0,), (0,)), ((), ())),
            precision=precision,
            preferred_element_type=f32,
        )

    def analysis_step(i, first):
        c = first + i
        matrix = transform[pl.ds(pl.multiple_of(i * MEMBERS, MEMBERS), MEMBERS), :]
        pieces = []
        for k in range(ROWS):
            value = background[c, k * MEMBERS : (k + 1) * MEMBERS, :].astype(f32)
            center = jnp.mean(value, axis=0, keepdims=True)
            pieces.append((center + apply(matrix, value - center)).astype(bf16))
        analysed = jnp.concatenate(pieces, axis=0)
        sent = jnp.dot(home[...], analysed, preferred_element_type=f32).astype(bf16)
        send3[c] = sent.reshape(GROUPS, LOCAL * ROWS, PLON)
        lanes = pl.ds(pl.multiple_of(c * PLON, PLON), PLON)
        for to in groups:
            remote(send3.at[c, to], out_hbm.at[g, :, lanes], 3, (to, b)).start()
        pltpu.make_async_copy(
            send3.at[c, g], out_hbm.at[g, :, lanes], local_sem.at[3]
        ).start()
        log_new[c] = jnp.exp(log_mean[c] + apply(matrix, log_spread[c], HI))
        return first

    def group_step(i, carry):
        first = i * TOGETHER
        lax.fori_loop(0, TOGETHER, background_step, first)
        solve()
        lax.fori_loop(0, TOGETHER, analysis_step, first)
        return carry

    lax.fori_loop(0, PATCHES // TOGETHER, group_step, 0)
    mult = log_new[...].reshape(PATCHES * MEMBERS, 128).astype(bf16)
    mult = jnp.dot(small[2], mult, preferred_element_type=f32)
    mult_send[...] = mult.reshape(GROUPS, pairs, 128)
    for to in groups:
        remote(mult_send.at[to], mult_in.at[g], 4, (to, b)).start()
    own_mult = pltpu.make_async_copy(mult_send.at[g], mult_in.at[g], local_sem.at[4])
    own_mult.start()

    own_mult.wait()
    wait_bytes(mult_in.at[pl.ds(0, GROUPS - 1)], recv_sem.at[4])
    mult = mult_in[...].reshape(GROUPS * pairs, 128).astype(bf16)
    mult = jnp.dot(small[3], mult, preferred_element_type=f32)
    mult_out[...] = mult.reshape(LOCAL, PATCHES, GROUPS, 128)[..., :REACTIONS].astype(bf16)
    wait_bytes(send3.at[:, 0], local_sem.at[3])
    wait_bytes(send3.at[:, pl.ds(0, GROUPS - 1)], recv_sem.at[3])
    wait_bytes(send1.at[pl.ds(0, BLOCKS - 1)], send_sem.at[0])
    wait_bytes(send1.at[0, pl.ds(0, LOCAL - 1)], send_sem.at[0])
    wait_bytes(send2.at[pl.ds(0, GROUPS * BANDS - 1)], send_sem.at[2])
    wait_bytes(send3.at[:, pl.ds(0, GROUPS - 1)], send_sem.at[3])
    wait_bytes(mult_send.at[pl.ds(0, GROUPS - 1)], send_sem.at[4])


def on_device(x, field, kinetic, cells, measured, variance):
    constants, final = tables()
    anywhere = pl.BlockSpec(memory_space=pl.ANY)
    vmem = pl.BlockSpec(memory_space=pltpu.VMEM)
    size = TOGETHER * MEMBERS
    pairs = LOCAL * PATCHES
    obs = cells.shape[-1]
    scratch = [
        pltpu.VMEM((LOCAL, TRACERS, BAND, NLON), f32),
        pltpu.VMEM((LOCAL * TRACERS * BAND, NLON), bf16),
        pltpu.VMEM((4, NLON, 256), bf16),
        pltpu.VMEM((PATCHES, 2 * NW, PLON), bf16),
        pltpu.VMEM((NW, NLAT), bf16),
        pltpu.VMEM((NLAT, NW), bf16),
        pltpu.VMEM((NW, 128), f32),
        pltpu.VMEM(constants[5].shape, bf16),
        pltpu.VMEM(constants[6].shape, bf16),
        pltpu.VMEM(constants[7].shape, bf16),
        pltpu.VMEM(constants[8].shape, bf16),
        pltpu.VMEM((LOCAL, PATCHES, GROUPS, REACTIONS), bf16),
        pltpu.VMEM((PATCHES, GROUPS, obs), jnp.int32),
        pltpu.VMEM((PATCHES, GROUPS, obs), f32),
        pltpu.VMEM((PATCHES, GROUPS, obs), f32),
        pltpu.VMEM((REACTIONS, BAND, NLON), bf16),
        pltpu.VMEM((REACTIONS, 8, NLON), f32),
        pltpu.VMEM((BLOCKS, LOCAL, TRACERS * BAND, 128), bf16),
        pltpu.VMEM((BANDS, TRACERS * BAND, 128), bf16),
        pltpu.VMEM((NLAT, TRACERS * 128), f32),
        pltpu.VMEM((NLAT, TRACERS * 128), bf16),
        pltpu.VMEM((NW, TRACERS * 128), bf16),
        pltpu.VMEM((GROUPS * BANDS, ROWS, 128), bf16),
        pltpu.VMEM((GROUPS, 2, BLOCKS, 2, ROWS, 128), bf16),
        pltpu.VMEM((MEMBERS, 16, BLOCKS * 128), f32),
        pltpu.VMEM((ROWS * MEMBERS, 2 * NW), bf16),
        pltpu.VMEM((GROUPS, pairs, 128), f32),
        pltpu.VMEM((GROUPS, pairs, 128), f32),
        pltpu.VMEM((PATCHES, REACTIONS, MEMBERS, 128), f32),
        pltpu.VMEM((PATCHES, MEMBERS, 128), f32),
        pltpu.VMEM((PATCHES, MEMBERS, 128), f32),
        pltpu.VMEM((PATCHES, MEMBERS, 128), f32),
        pltpu.VMEM((PATCHES, ROWS * MEMBERS, PLON), bf16),
        pltpu.VMEM((size, 128), f32),
        pltpu.VMEM((size, 128), f32),
        pltpu.VMEM((size, 128), f32),
        pltpu.VMEM((size, MEMBERS), f32),
        pltpu.VMEM((PATCHES, GROUPS, LOCAL * ROWS, PLON), bf16),
        pltpu.VMEM((GROUPS, pairs, 128), f32),
        pltpu.VMEM((GROUPS, pairs, 128), f32),
        pltpu.SemaphoreType.DMA((18,)),
        pltpu.SemaphoreType.DMA((5,)),
        pltpu.SemaphoreType.DMA((5,)),
        pltpu.SemaphoreType.DMA((5,)),
        pltpu.SemaphoreType.REGULAR,
    ]
    out, mult = pl.pallas_call(
        kernel,
        out_shape=(
            jax.ShapeDtypeStruct((GROUPS, LOCAL * ROWS, NLON), bf16),
            jax.ShapeDtypeStruct((LOCAL, PATCHES, GROUPS, REACTIONS), bf16),
        ),
        in_specs=[anywhere] * (6 + len(constants)),
        out_specs=(anywhere, vmem),
        scratch_shapes=scratch,
        compiler_params=pltpu.CompilerParams(
            collective_id=0, has_side_effects=True, vmem_limit_bytes=60 << 20
        ),
        name="assimilate",
    )(
        x,
        field,
        kinetic.transpose(0, 3, 2, 1),
        cells.transpose(1, 0, 2),
        measured.transpose(1, 0, 2),
        variance.transpose(1, 0, 2),
        *constants,
    )
    analysis = jnp.dot(
        final, out.reshape(GROUPS * LOCAL * ROWS, NLON), preferred_element_type=f32
    ).astype(bf16)
    return analysis.reshape(LOCAL, TRACERS, BAND, NLON), mult.transpose(0, 3, 2, 1)


def solution(mesh):
    return jax.shard_map(
        on_device,
        mesh=mesh,
        in_specs=(
            P("mem", None, "grid", None),
            P(None, "grid", None),
            P("mem", None, "grid", None),
            P("grid", None, None),
            P("grid", None, None),
            P("grid", None, None),
        ),
        out_specs=(P("mem", None, "grid", None), P("mem", None, "grid", None)),
        check_vma=False,
    )
```

```python
import functools
import math

import jax
import jax.numpy as jnp
import ml_dtypes
import numpy as np
from jax import lax
from jax.experimental import pallas as pl
from jax.experimental.pallas import tpu as pltpu
from jax.sharding import PartitionSpec as P

NLAT = 768
NLON = 1536
NW = 512
PLAT = 3
PLON = 256
SWEEPS = 5
TRACERS = 4
MEMBERS = 32
REACTIONS = 12
DAMPING = 2.0

GROUPS = 8
BANDS = 32
LOCAL = 4
BLOCKS = 8
TOGETHER = (3, 3)
BAND = NLAT // BANDS
PATCHES = NLON // PLON
ROWS = TRACERS * PLAT
MESH = pl.DeviceIdType.MESH
HI = lax.Precision.HIGHEST

PAIRS = ((1, 1), (0, 1), (1, 0), (0, 0))
ZSTEPS = (4, 3, 5, 2, 6, 1, 7, 0)

f32 = jnp.float32
bf16 = jnp.bfloat16


def wave_numbers():
    block = np.arange(BLOCKS)[:, None]
    place = np.arange(NW // BLOCKS)[None, :]
    return 2 * ((block // 2) * (NW // BLOCKS) + place) + block % 2


@functools.lru_cache(maxsize=1)
def tables():
    waves = wave_numbers()
    m = waves.reshape(-1)
    phase = (m[:, None] * np.arange(NLON)[None, :]) % NLON
    angle = phase.astype(np.float32) * np.float32(2.0 * math.pi / NLON)
    cosine, sine = np.cos(angle), np.sin(angle)
    forward = np.stack([cosine, -sine], axis=1).reshape(2 * NW, NLON).T
    forward = forward.reshape(NLON, 4, 256).transpose(1, 0, 2)
    weight = np.where(m == 0, 1.0, 2.0).astype(np.float32)[:, None]
    inverse = np.stack([weight * cosine, -weight * sine], axis=1).reshape(2 * NW, NLON)
    inverse = inverse.reshape(2 * NW, PATCHES, PLON).transpose(1, 0, 2)

    order = np.arange(NW, dtype=np.float32)
    theta = (np.arange(NLAT, dtype=np.float32) + np.float32(0.5)) * np.float32(math.pi / NLAT)
    even = np.cos(theta[:, None] * order[None, :])
    odd = np.sin(theta[:, None] * (order[None, :] + np.float32(1.0)))
    both = np.stack([even, odd])
    to_modes = both.transpose(0, 2, 1)
    dest = np.arange(GROUPS)[:, None, None], np.arange(BANDS)[None, :, None], np.arange(PLAT)
    rows = (dest[1] * BAND + dest[0] * PLAT + dest[2]).reshape(-1)
    to_rows = both[:, rows, :]

    total = (waves[:, None, :] + np.arange(NW)[None, :, None]).astype(np.float32)
    ratio = total * (total + np.float32(1.0)) / np.float32(NW * (NW - 1))
    half = np.where((waves[:, None, :] % 2 == 0) & (np.arange(NW)[None, :, None] == 0), 0.5, 1.0)
    gain = (half / (1.0 + DAMPING * ratio * ratio)).astype(np.float32) * np.float32(2.0 / NLAT)
    gain = np.where(total <= NW - 1, gain, 0.0).astype(np.float32)
    gain = np.repeat(gain, 2, axis=2)

    spread = np.zeros((BANDS, 16, TRACERS, BANDS, PLAT), np.float32)
    for b in range(BANDS):
        for t in range(TRACERS):
            for j in range(PLAT):
                spread[b, t * PLAT + j, t, b, j] = 1.0
    spread = spread.reshape(BANDS * 16, TRACERS * BANDS * PLAT)
    gather = np.zeros((ROWS, MEMBERS, MEMBERS, 16), np.float32)
    for e in range(MEMBERS):
        for a in range(ROWS):
            gather[a, e, e, a] = 1.0
    gather = gather.reshape(ROWS * MEMBERS, MEMBERS * 16)
    home = np.zeros((GROUPS, LOCAL, ROWS, ROWS, GROUPS, LOCAL), np.float32)
    for g in range(GROUPS):
        for e in range(LOCAL):
            for a in range(ROWS):
                home[g, e, a, a, g, e] = 1.0
    home = home.reshape(MEMBERS * ROWS, ROWS * MEMBERS)
    index = np.arange(LOCAL * PATCHES * GROUPS)
    e, c, g = np.unravel_index(index, (LOCAL, PATCHES, GROUPS))
    by_group = np.zeros((index.size, index.size), np.float32)
    by_group[(g * LOCAL + e) * PATCHES + c, index] = 1.0
    g, e, c = np.unravel_index(index, (GROUPS, LOCAL, PATCHES))
    by_patch = np.zeros((index.size, index.size), np.float32)
    by_patch[(c * GROUPS + g) * LOCAL + e, index] = 1.0
    small = np.stack([by_group, by_patch, by_patch.T, by_group.T])
    index = np.arange(GROUPS * LOCAL * ROWS)
    g, et, j = np.unravel_index(index, (GROUPS, LOCAL * TRACERS, PLAT))
    final = np.zeros((index.size, index.size), np.float32)
    final[(et * GROUPS + g) * PLAT + j, index] = 1.0
    b = lambda v: np.asarray(v, np.float32).astype(ml_dtypes.bfloat16)
    return (b(forward), b(inverse), b(to_modes), b(to_rows), gain) + (
        b(spread),
        b(gather),
        b(home),
        b(small),
        b(final),
    )


def split_grid(b):
    return b // 16, lax.rem(b // 2, 8), lax.rem(b, 2)


def wrap(value, size):
    return jnp.where(value >= size, value - size, value)


def kernel(
    x_hbm,
    field_hbm,
    fac_hbm,
    cells_hbm,
    measured_hbm,
    variance_hbm,
    forward_hbm,
    inverse_hbm,
    modes_hbm,
    rows_hbm,
    gain_hbm,
    spread_hbm,
    gather_hbm,
    home_hbm,
    small_hbm,
    final_hbm,
    out_hbm,
    mult_out,
    x,
    xb,
    forward,
    inverse,
    modes,
    rows,
    gain,
    spread,
    gather,
    home,
    small,
    final,
    fac_raw,
    cells,
    measured,
    variance,
    field,
    field_rows,
    send1,
    recv1,
    staged,
    plane,
    damped,
    send2,
    recv2,
    padded,
    coefficients,
    fac,
    fac_in,
    fac_wide,
    mix,
    log_mean,
    log_spread,
    log_new,
    background,
    weighted,
    spread_seen,
    projected,
    transform,
    send3,
    recv3,
    result,
    mult_send,
    mult_in,
    load_sem,
    local_sem,
    send_sem,
    recv_sem,
    patch_sem,
    pair_sem,
    ready,
):
    g, b = lax.axis_index("mem"), lax.axis_index("grid")
    half, z, core = split_grid(b)
    member = half * 2 + core

    def load(src, dst, i):
        return pltpu.make_async_copy(src, dst, load_sem.at[i])

    load_x = load(x_hbm, x, 0)
    load_x.start()
    load_fac = [load(fac_hbm, fac_raw, 13), load(small_hbm, small, 14)]
    for one in load_fac:
        one.start()
    load_forward = [load(forward_hbm.at[i], forward.at[i], 1 + i) for i in range(4)]
    for one in load_forward:
        one.start()
    parity = lax.rem(z, 2)
    later = [
        load(modes_hbm.at[parity], modes, 5),
        load(rows_hbm.at[parity], rows, 6),
        load(gain_hbm.at[z], gain, 7),
        load(spread_hbm, spread, 8),
        load(field_hbm, field, 9),
        load(inverse_hbm, inverse, 10),
        load(gather_hbm, gather, 11),
        load(home_hbm, home, 12),
        load(final_hbm, final, 18),
        load(cells_hbm, cells, 15),
        load(measured_hbm, measured, 16),
        load(variance_hbm, variance, 17),
    ]

    barrier = pltpu.get_barrier_semaphore()

    groups = [wrap(g + step, GROUPS) for step in range(1, GROUPS)]
    bands = [
        wrap(half + a, 2) * 16 + wrap(z + dz, BLOCKS) * 2 + wrap(core + c, 2)
        for a, c in PAIRS
        for dz in ZSTEPS
        if a or c or dz
    ]
    for to in groups:
        pl.semaphore_signal(barrier, inc=1, device_id=(to, b), device_id_type=MESH)
    for to in bands:
        pl.semaphore_signal(barrier, inc=1, device_id=(g, to), device_id_type=MESH)

    def remote(src, dst, i, to):
        return pltpu.make_async_remote_copy(
            src_ref=src,
            dst_ref=dst,
            send_sem=send_sem.at[i],
            recv_sem=recv_sem.at[i],
            device_id=to,
            device_id_type=MESH,
        )

    def wait_bytes(ref, sem):
        pltpu.make_async_copy(ref, ref, sem).wait()

    load_x.wait()
    xb[...] = x[...].reshape(LOCAL * TRACERS * BAND, NLON).astype(bf16)
    for one in load_forward:
        one.wait()
    for one in later:
        one.start()

    def forward_step(i, carry):
        value = jnp.dot(xb[...], forward[i], preferred_element_type=f32) * (1.0 / NLON)
        value = value.astype(bf16).reshape(LOCAL, TRACERS * BAND, 256)
        send1[2 * i] = value[:, :, :128]
        send1[2 * i + 1] = value[:, :, 128:]
        return carry

    lax.fori_loop(0, 4, forward_step, 0)
    pl.semaphore_wait(barrier, GROUPS + BANDS - 2)
    for to in groups:
        pl.semaphore_signal(ready, inc=1, device_id=(to, b), device_id_type=MESH)
    for band in bands:
        h2, z2, c2 = split_grid(band)
        remote(send1.at[z2, h2 * 2 + c2], recv1.at[b], 0, (g, band)).start()
    own1 = pltpu.make_async_copy(send1.at[z, member], recv1.at[b], local_sem.at[0])
    own1.start()
    pairs = LOCAL * PATCHES
    for one in load_fac:
        one.wait()
    raw = fac_raw[...].astype(f32).reshape(pairs * GROUPS, REACTIONS).astype(bf16)
    fac[...] = jnp.ones(fac.shape, f32)
    raw = jnp.dot(small[0], raw, preferred_element_type=f32)
    fac[:, :, :REACTIONS] = raw.reshape(GROUPS, pairs, REACTIONS)
    for to in groups:
        remote(fac.at[to], fac_in.at[g], 1, (to, b)).start()
    own_fac = pltpu.make_async_copy(fac.at[g], fac_in.at[g], local_sem.at[1])
    own_fac.start()

    for one in later:
        one.wait()
    padded[...] = jnp.zeros(padded.shape, bf16)

    line_of = lax.broadcasted_iota(jnp.int32, (8, BAND), 0) + g * PLAT
    own_lines = jnp.where(line_of == lax.broadcasted_iota(jnp.int32, (8, BAND), 1), 1.0, 0.0)
    own_lines = own_lines.astype(bf16)

    def widen(r, carry):
        field_rows[r] = jnp.dot(own_lines, field[r], preferred_element_type=f32)
        return carry

    lax.fori_loop(0, REACTIONS, widen, 0)
    own_fac.wait()
    wait_bytes(fac_in.at[pl.ds(0, GROUPS - 1)], recv_sem.at[1])
    wait_bytes(fac.at[pl.ds(0, GROUPS - 1)], send_sem.at[1])
    factors = jnp.dot(
        small[1],
        fac_in[...].reshape(GROUPS * pairs, 128).astype(bf16),
        preferred_element_type=f32,
    )
    for c in range(PATCHES):
        for r in range(REACTIONS):
            column = factors[c * MEMBERS : (c + 1) * MEMBERS, r : r + 1]
            fac_wide[c, r] = jnp.broadcast_to(column, (MEMBERS, 128))
    log_rate = jnp.log(factors).reshape(PATCHES, MEMBERS, 128)
    log_mean[...] = jnp.broadcast_to(
        jnp.mean(log_rate, axis=1, keepdims=True), (PATCHES, MEMBERS, 128)
    )
    log_spread[...] = log_rate - log_mean[...]

    own1.wait()
    wait_bytes(recv1.at[pl.ds(0, BANDS - 1)], recv_sem.at[0])

    def unpack(s, carry):
        value = recv1[s].astype(f32)
        at = pl.ds(pl.multiple_of(s * BAND, 8), BAND)
        for t in range(TRACERS):
            staged[at, t * 128 : (t + 1) * 128] = value[t * BAND : (t + 1) * BAND]
        return carry

    lax.fori_loop(0, BANDS, unpack, 0)
    plane[...] = staged[...].astype(bf16)

    def to_modes(i, carry):
        at = pl.ds(pl.multiple_of(i * 128, 128), 128)
        value = jnp.dot(modes[at, :], plane[...], preferred_element_type=f32)
        scale = gain[at, :]
        for t in range(TRACERS):
            lanes = slice(t * 128, (t + 1) * 128)
            damped[at, lanes] = (value[:, lanes] * scale).astype(bf16)
        return carry

    lax.fori_loop(0, NW // 128, to_modes, 0)

    def to_owner(step, carry):
        owner = wrap(g + step, GROUPS)
        at = pl.ds(pl.multiple_of(owner * 96, 32), 96)
        value = jnp.dot(rows[at, :], damped[...], preferred_element_type=f32).astype(bf16)
        stacked = jnp.concatenate([value[:, t * 128 : (t + 1) * 128] for t in range(TRACERS)], 0)
        wide = jnp.dot(spread[...], stacked, preferred_element_type=f32)
        wide = wide.reshape(BANDS, 16, 128).astype(bf16)
        send2[pl.ds(owner * BANDS, BANDS)] = wide[:, :ROWS]
        push(step, owner, 0)
        return carry

    def push(step, owner, to_core):
        for a in (1, 0):
            for dz in ZSTEPS:
                band = wrap(half + a, 2) * 16 + wrap(z + dz, BLOCKS) * 2 + to_core
                copy = pltpu.make_async_remote_copy(
                    src_ref=send2.at[owner * BANDS + band],
                    dst_ref=recv2.at[g, half, z, core],
                    send_sem=send_sem.at[2],
                    recv_sem=pair_sem.at[z // 2],
                    device_id=(owner, band),
                    device_id_type=MESH,
                )
                if a or dz:
                    copy.start()
                else:
                    pl.when(jnp.logical_or(step != 0, core != to_core))(copy.start)

    def push_rest(step, carry):
        push(step, wrap(g + step, GROUPS), 1)
        return carry

    def reaction_step(c, carry):
        for j in range(PLAT):
            for h in range(PLON // 128):
                lanes = pl.ds(pl.multiple_of(c * PLON + h * 128, 128), 128)
                rates = [fac_wide[c, r] * field_rows[r, j : j + 1, lanes] for r in range(REACTIONS)]
                for s in range(TRACERS):
                    outflow = rates[3 * s] + rates[3 * s + 1] + rates[3 * s + 2]
                    leave = 1.0 / (1.0 + outflow)
                    mix[c, j, h, s, s] = leave
                    for t in range(TRACERS):
                        if t != s:
                            mix[c, j, h, t, s] = rates[3 * s + (t if t < s else t - 1)] * leave
        return carry

    pl.semaphore_wait(ready, GROUPS - 1)
    lax.fori_loop(0, GROUPS, to_owner, 0)
    lax.fori_loop(0, GROUPS, push_rest, 0)
    own2 = pltpu.make_async_copy(
        send2.at[g * BANDS + b], recv2.at[g, half, z, core], pair_sem.at[z // 2]
    )
    own2.start()
    lax.fori_loop(0, PATCHES, reaction_step, 0)

    for i in range(BLOCKS // 2):
        wait_bytes(recv2.at[:, :, pl.ds(2 * i, 2)], pair_sem.at[i])
        for block in (2 * i, 2 * i + 1):
            value = recv2[:, :, block, :, :, :].reshape(MEMBERS, ROWS, 128)
            padded[:, :ROWS, block * 128 : (block + 1) * 128] = value
        lanes = slice(i * 256, (i + 1) * 256)
        value = padded[:, :, lanes].reshape(MEMBERS * 16, 256)
        coefficients[:, lanes] = jnp.dot(
            gather[...], value, preferred_element_type=f32
        ).astype(bf16)

    obs = cells.shape[-1]

    def background_step(c):
        smooth = jnp.dot(coefficients[...], inverse[c], preferred_element_type=f32)
        smooth = smooth.reshape(TRACERS, PLAT, MEMBERS, PLON)
        for j in range(PLAT):
            for h in range(PLON // 128):
                tracers = [smooth[t, j, :, h * 128 : (h + 1) * 128] for t in range(TRACERS)]
                for t in range(TRACERS):
                    value = mix[c, j, h, t, t] * tracers[t]
                    for s in range(TRACERS):
                        if s != t:
                            value = value + mix[c, j, h, t, s] * tracers[s]
                    row = (t * PLAT + j) * MEMBERS
                    background[c, row : row + MEMBERS, h * 128 : (h + 1) * 128] = value.astype(
                        bf16
                    )
        cell = cells[c, pl.ds(g, 1), :]
        column = jnp.bitwise_and(cell, PLON - 1)
        row = lax.shift_right_logical(cell, 8)
        picker = jnp.where(
            lax.broadcasted_iota(jnp.int32, (PLON, obs), 0) == column, 1.0, 0.0
        ).astype(bf16)
        seen = jnp.dot(background[c], picker, preferred_element_type=f32)
        predicted = jnp.zeros((MEMBERS, obs), f32)
        for k in range(ROWS):
            predicted = predicted + jnp.where(
                row == k, seen[k * MEMBERS : (k + 1) * MEMBERS], 0.0
            )
        seen_mean = jnp.mean(predicted, axis=0, keepdims=True)
        spread_of = predicted - seen_mean
        weight = spread_of * (1.0 / variance[c, pl.ds(g, 1), :])
        innovation = measured[c, pl.ds(g, 1), :] - seen_mean
        at = pl.ds(c * MEMBERS, MEMBERS)
        weighted[at, :] = weight
        spread_seen[at, :] = spread_of
        projected[at, :] = jnp.broadcast_to(
            jnp.sum(weight * innovation, axis=1, keepdims=True), (MEMBERS, 128)
        )

    def halves(value):
        high = value.astype(bf16)
        return high, (value - high.astype(f32)).astype(bf16)

    def exact(left, right):
        (a, b), (c, d) = halves(left), halves(right)
        dot = functools.partial(jnp.dot, preferred_element_type=f32)
        return dot(a, c) + (dot(a, d) + dot(b, c))

    def solve(first, last):
        size = (last - first) * MEMBERS
        at = slice(first * MEMBERS, last * MEMBERS)
        block_row = lax.broadcasted_iota(jnp.int32, (size, size), 0)
        block_col = lax.broadcasted_iota(jnp.int32, (size, size), 1)
        same = block_row // MEMBERS == block_col // MEMBERS
        identity = jnp.where(block_row == block_col, 1.0, 0.0)
        outer = lax.dot_general(
            weighted[at, :],
            spread_seen[at, :],
            (((1,), (1,)), ((), ())),
            precision=HI,
            preferred_element_type=f32,
        )
        outer = jnp.where(same, outer, 0.0)
        square = jnp.sum(outer * outer, axis=1, keepdims=True).reshape(last - first, MEMBERS, 1)
        square = jnp.broadcast_to(jnp.sum(square, axis=1, keepdims=True), (last - first, MEMBERS, 1))
        scale = (MEMBERS - 1.0) + jnp.sqrt(square.reshape(size, 1))
        current = ((MEMBERS - 1.0) * identity + outer) / scale
        root = 1.5 * identity - 0.5 * current
        current = exact(current, root)
        for sweep in range(1, SWEEPS):
            middle = 1.5 * identity - 0.5 * exact(root, current)
            if sweep < SWEEPS - 1:
                current = exact(current, middle)
            root = exact(middle, root)
        mean_weight = exact(root, exact(root, projected[at, :])) / scale
        full = jnp.where(same, jnp.sqrt((MEMBERS - 1.0) / scale) * root, 0.0)
        fold = jnp.where(
            lax.rem(lax.broadcasted_iota(jnp.int32, (size, MEMBERS), 0), MEMBERS)
            == lax.broadcasted_iota(jnp.int32, (size, MEMBERS), 1),
            1.0,
            0.0,
        )
        transform[at, :] = exact(full, fold) + mean_weight[:, :MEMBERS]

    def apply(matrix, values, precision=None):
        return lax.dot_general(
            matrix,
            values,
            (((0,), (0,)), ((), ())),
            precision=precision,
            preferred_element_type=f32,
        )

    def analysis_step(c):
        matrix = transform[c * MEMBERS : (c + 1) * MEMBERS, :]
        pieces = []
        for k in range(ROWS):
            value = background[c, k * MEMBERS : (k + 1) * MEMBERS, :].astype(f32)
            center = jnp.mean(value, axis=0, keepdims=True)
            pieces.append((center + apply(matrix, value - center)).astype(bf16))
        analysed = jnp.concatenate(pieces, axis=0)
        sent = jnp.dot(home[...], analysed, preferred_element_type=f32).astype(bf16)
        send3[c] = sent.reshape(GROUPS, LOCAL * ROWS, PLON)
        for to in groups:
            pltpu.make_async_remote_copy(
                src_ref=send3.at[c, to],
                dst_ref=recv3.at[c, g],
                send_sem=send_sem.at[3],
                recv_sem=patch_sem.at[c],
                device_id=(to, b),
                device_id_type=MESH,
            ).start()
        recv3[c, g] = send3[c, g]

    def multipliers(c):
        matrix = transform[c * MEMBERS : (c + 1) * MEMBERS, :]
        log_new[c] = jnp.exp(log_mean[c] + apply(matrix, log_spread[c], HI))

    def finish(first, last):
        for c in range(first, last):
            multipliers(c)
        if last == PATCHES:
            send_multipliers()
        for c in range(first, last):
            analysis_step(c)

    own_mult = pltpu.make_async_copy(mult_send.at[g], mult_in.at[g], local_sem.at[4])

    def send_multipliers():
        mult = log_new[...].reshape(PATCHES * MEMBERS, 128).astype(bf16)
        mult = jnp.dot(small[2], mult, preferred_element_type=f32)
        mult_send[...] = mult.reshape(GROUPS, pairs, 128)
        for to in groups:
            remote(mult_send.at[to], mult_in.at[g], 4, (to, b)).start()
        own_mult.start()

    first = 0
    for count in TOGETHER:
        last = first + count
        for c in range(first, last):
            background_step(c)
        if first:
            finish(before, first)
        solve(first, last)
        before, first = first, last
    finish(before, first)
    own_mult.wait()
    wait_bytes(mult_in.at[pl.ds(0, GROUPS - 1)], recv_sem.at[4])
    mult = mult_in[...].reshape(GROUPS * pairs, 128).astype(bf16)
    mult = jnp.dot(small[3], mult, preferred_element_type=f32)
    mult_out[...] = mult.reshape(LOCAL, PATCHES, GROUPS, 128)[..., :REACTIONS].astype(bf16)

    def store(c):
        lanes = pl.ds(pl.multiple_of(c * PLON, PLON), PLON)
        return pltpu.make_async_copy(result.at[:, lanes], out_hbm.at[:, lanes], local_sem.at[3])

    def final_step(c, carry):
        wait_bytes(recv3.at[c, pl.ds(0, GROUPS - 1)], patch_sem.at[c])
        lanes = pl.ds(pl.multiple_of(c * PLON, PLON), PLON)
        value = recv3[c].reshape(GROUPS * LOCAL * ROWS, PLON)
        result[:, lanes] = jnp.dot(final[...], value, preferred_element_type=f32).astype(bf16)
        store(c).start()
        return carry

    lax.fori_loop(0, PATCHES, final_step, 0)
    wait_bytes(result, local_sem.at[3])
    wait_bytes(send1.at[pl.ds(0, BLOCKS - 1)], send_sem.at[0])
    wait_bytes(send1.at[0, pl.ds(0, LOCAL - 1)], send_sem.at[0])
    wait_bytes(send2.at[pl.ds(0, GROUPS * BANDS - 1)], send_sem.at[2])
    wait_bytes(send3.at[:, pl.ds(0, GROUPS - 1)], send_sem.at[3])
    wait_bytes(mult_send.at[pl.ds(0, GROUPS - 1)], send_sem.at[4])


def keep(values, mult, out, mult_out, held, mult_held, in_sem, out_sem):
    pieces = [(mult, mult_held, mult_out)]
    for i in range(8):
        at = pl.ds(i * 48, 48)
        pieces.append((values.at[at], held.at[at], out.at[at]))
    reads = [pltpu.make_async_copy(a, b, in_sem.at[i]) for i, (a, b, _) in enumerate(pieces)]
    writes = [pltpu.make_async_copy(b, c, out_sem.at[i]) for i, (_, b, c) in enumerate(pieces)]
    for read in reads:
        read.start()
    for read, write in zip(reads, writes):
        read.wait()
        write.start()
    for write in writes:
        write.wait()


def on_device(x, field, kinetic, cells, measured, variance):
    constants = tables()
    anywhere = pl.BlockSpec(memory_space=pl.ANY)
    vmem = pl.BlockSpec(memory_space=pltpu.VMEM)
    size = PATCHES * MEMBERS
    pairs = LOCAL * PATCHES
    obs = cells.shape[-1]
    scratch = [
        pltpu.VMEM((LOCAL, TRACERS, BAND, NLON), f32),
        pltpu.VMEM((LOCAL * TRACERS * BAND, NLON), bf16),
        pltpu.VMEM((4, NLON, 256), bf16),
        pltpu.VMEM((PATCHES, 2 * NW, PLON), bf16),
        pltpu.VMEM((NW, NLAT), bf16),
        pltpu.VMEM((NLAT, NW), bf16),
        pltpu.VMEM((NW, 128), f32),
        pltpu.VMEM(constants[5].shape, bf16),
        pltpu.VMEM(constants[6].shape, bf16),
        pltpu.VMEM(constants[7].shape, bf16),
        pltpu.VMEM(constants[8].shape, bf16),
        pltpu.VMEM(constants[9].shape, bf16),
        pltpu.VMEM((LOCAL, PATCHES, GROUPS, REACTIONS), bf16),
        pltpu.VMEM((PATCHES, GROUPS, obs), jnp.int32),
        pltpu.VMEM((PATCHES, GROUPS, obs), f32),
        pltpu.VMEM((PATCHES, GROUPS, obs), f32),
        pltpu.VMEM((REACTIONS, BAND, NLON), bf16),
        pltpu.VMEM((REACTIONS, 8, NLON), f32),
        pltpu.VMEM((BLOCKS, LOCAL, TRACERS * BAND, 128), bf16),
        pltpu.VMEM((BANDS, TRACERS * BAND, 128), bf16),
        pltpu.VMEM((NLAT, TRACERS * 128), f32),
        pltpu.VMEM((NLAT, TRACERS * 128), bf16),
        pltpu.VMEM((NW, TRACERS * 128), bf16),
        pltpu.VMEM((GROUPS * BANDS, ROWS, 128), bf16),
        pltpu.VMEM((GROUPS, 2, BLOCKS, 2, ROWS, 128), bf16),
        pltpu.VMEM((MEMBERS, 16, BLOCKS * 128), bf16),
        pltpu.VMEM((ROWS * MEMBERS, 2 * NW), bf16),
        pltpu.VMEM((GROUPS, pairs, 128), f32),
        pltpu.VMEM((GROUPS, pairs, 128), f32),
        pltpu.VMEM((PATCHES, REACTIONS, MEMBERS, 128), f32),
        pltpu.VMEM((PATCHES, PLAT, 2, TRACERS, TRACERS, MEMBERS, 128), f32),
        pltpu.VMEM((PATCHES, MEMBERS, 128), f32),
        pltpu.VMEM((PATCHES, MEMBERS, 128), f32),
        pltpu.VMEM((PATCHES, MEMBERS, 128), f32),
        pltpu.VMEM((PATCHES, ROWS * MEMBERS, PLON), bf16),
        pltpu.VMEM((size, 128), f32),
        pltpu.VMEM((size, 128), f32),
        pltpu.VMEM((size, 128), f32),
        pltpu.VMEM((size, MEMBERS), f32),
        pltpu.VMEM((PATCHES, GROUPS, LOCAL * ROWS, PLON), bf16),
        pltpu.VMEM((PATCHES, GROUPS, LOCAL * ROWS, PLON), bf16),
        pltpu.VMEM((LOCAL * TRACERS * BAND, NLON), bf16),
        pltpu.VMEM((GROUPS, pairs, 128), f32),
        pltpu.VMEM((GROUPS, pairs, 128), f32),
        pltpu.SemaphoreType.DMA((19,)),
        pltpu.SemaphoreType.DMA((5,)),
        pltpu.SemaphoreType.DMA((5,)),
        pltpu.SemaphoreType.DMA((5,)),
        pltpu.SemaphoreType.DMA((PATCHES,)),
        pltpu.SemaphoreType.DMA((BLOCKS // 2,)),
        pltpu.SemaphoreType.REGULAR,
    ]
    out, mult = pl.pallas_call(
        kernel,
        out_shape=(
            jax.ShapeDtypeStruct((LOCAL * TRACERS * BAND, NLON), bf16),
            jax.ShapeDtypeStruct((LOCAL, PATCHES, GROUPS, REACTIONS), bf16),
        ),
        in_specs=[anywhere] * (6 + len(constants)),
        out_specs=(anywhere, vmem),
        scratch_shapes=scratch,
        compiler_params=pltpu.CompilerParams(
            collective_id=0, has_side_effects=True, vmem_limit_bytes=60 << 20
        ),
        name="assimilate",
    )(
        x,
        field,
        kinetic.transpose(0, 3, 2, 1),
        cells.transpose(1, 0, 2),
        measured.transpose(1, 0, 2),
        variance.transpose(1, 0, 2),
        *constants,
    )
    out, mult = pl.pallas_call(
        keep,
        out_shape=(
            jax.ShapeDtypeStruct(out.shape, bf16),
            jax.ShapeDtypeStruct(mult.shape, bf16),
        ),
        in_specs=[anywhere] * 2,
        out_specs=(anywhere,) * 2,
        scratch_shapes=[
            pltpu.VMEM(out.shape, bf16),
            pltpu.VMEM(mult.shape, bf16),
            pltpu.SemaphoreType.DMA((9,)),
            pltpu.SemaphoreType.DMA((9,)),
        ],
        compiler_params=pltpu.CompilerParams(vmem_limit_bytes=60 << 20),
        name="keep",
    )(out, mult)
    return out.reshape(LOCAL, TRACERS, BAND, NLON), mult.transpose(0, 3, 2, 1)


def solution(mesh):
    return jax.shard_map(
        on_device,
        mesh=mesh,
        in_specs=(
            P("mem", None, "grid", None),
            P(None, "grid", None),
            P("mem", None, "grid", None),
            P("grid", None, None),
            P("grid", None, None),
            P("grid", None, None),
        ),
        out_specs=(P("mem", None, "grid", None), P("mem", None, "grid", None)),
        check_vma=False,
    )
```

```python
import functools
import math

import jax
import jax.numpy as jnp
import ml_dtypes
import numpy as np
from jax import lax
from jax.experimental import pallas as pl
from jax.experimental.pallas import tpu as pltpu
from jax.sharding import PartitionSpec as P

NLAT = 768
NLON = 1536
NW = 512
PLAT = 3
PLON = 256
SWEEPS = 5
TRACERS = 4
MEMBERS = 32
REACTIONS = 12
DAMPING = 2.0

GROUPS = 8
BANDS = 32
LOCAL = 4
BLOCKS = 8
TOGETHER = (4, 2)
BAND = NLAT // BANDS
PATCHES = NLON // PLON
ROWS = TRACERS * PLAT
MESH = pl.DeviceIdType.MESH
HI = lax.Precision.HIGHEST

PAIRS = ((1, 1), (0, 1), (1, 0), (0, 0))
ZSTEPS = (4, 3, 5, 2, 6, 1, 7, 0)

f32 = jnp.float32
bf16 = jnp.bfloat16


def wave_numbers():
    block = np.arange(BLOCKS)[:, None]
    place = np.arange(NW // BLOCKS)[None, :]
    return 2 * ((block // 2) * (NW // BLOCKS) + place) + block % 2


@functools.lru_cache(maxsize=1)
def tables():
    waves = wave_numbers()
    m = waves.reshape(-1)
    phase = (m[:, None] * np.arange(NLON)[None, :]) % NLON
    angle = phase.astype(np.float32) * np.float32(2.0 * math.pi / NLON)
    cosine, sine = np.cos(angle), np.sin(angle)
    forward = np.stack([cosine, -sine], axis=1).reshape(2 * NW, NLON).T
    forward = forward.reshape(NLON, 4, 256).transpose(1, 0, 2)
    weight = np.where(m == 0, 1.0, 2.0).astype(np.float32)[:, None]
    inverse = np.stack([weight * cosine, -weight * sine], axis=1).reshape(2 * NW, NLON)
    inverse = inverse.reshape(2 * NW, PATCHES, PLON).transpose(1, 0, 2)

    order = np.arange(NW, dtype=np.float32)
    theta = (np.arange(NLAT, dtype=np.float32) + np.float32(0.5)) * np.float32(math.pi / NLAT)
    even = np.cos(theta[:, None] * order[None, :])
    odd = np.sin(theta[:, None] * (order[None, :] + np.float32(1.0)))
    both = np.stack([even, odd])
    to_modes = both.transpose(0, 2, 1)
    dest = np.arange(GROUPS)[:, None, None], np.arange(BANDS)[None, :, None], np.arange(PLAT)
    rows = (dest[1] * BAND + dest[0] * PLAT + dest[2]).reshape(-1)
    to_rows = both[:, rows, :]

    total = (waves[:, None, :] + np.arange(NW)[None, :, None]).astype(np.float32)
    ratio = total * (total + np.float32(1.0)) / np.float32(NW * (NW - 1))
    half = np.where((waves[:, None, :] % 2 == 0) & (np.arange(NW)[None, :, None] == 0), 0.5, 1.0)
    gain = (half / (1.0 + DAMPING * ratio * ratio)).astype(np.float32) * np.float32(2.0 / NLAT)
    gain = np.where(total <= NW - 1, gain, 0.0).astype(np.float32)
    gain = np.repeat(gain, 2, axis=2)

    spread = np.zeros((BANDS, 16, TRACERS, BANDS, PLAT), np.float32)
    for b in range(BANDS):
        for t in range(TRACERS):
            for j in range(PLAT):
                spread[b, t * PLAT + j, t, b, j] = 1.0
    spread = spread.reshape(BANDS * 16, TRACERS * BANDS * PLAT)
    gather = np.zeros((ROWS, MEMBERS, MEMBERS, 16), np.float32)
    for e in range(MEMBERS):
        for a in range(ROWS):
            gather[a, e, e, a] = 1.0
    gather = gather.reshape(ROWS * MEMBERS, MEMBERS * 16)
    home = np.zeros((GROUPS, LOCAL, ROWS, ROWS, GROUPS, LOCAL), np.float32)
    for g in range(GROUPS):
        for e in range(LOCAL):
            for a in range(ROWS):
                home[g, e, a, a, g, e] = 1.0
    home = home.reshape(MEMBERS * ROWS, ROWS * MEMBERS)
    index = np.arange(LOCAL * PATCHES * GROUPS)
    e, c, g = np.unravel_index(index, (LOCAL, PATCHES, GROUPS))
    by_group = np.zeros((index.size, index.size), np.float32)
    by_group[(g * LOCAL + e) * PATCHES + c, index] = 1.0
    g, e, c = np.unravel_index(index, (GROUPS, LOCAL, PATCHES))
    by_patch = np.zeros((index.size, index.size), np.float32)
    by_patch[(c * GROUPS + g) * LOCAL + e, index] = 1.0
    small = np.stack([by_group, by_patch, by_patch.T, by_group.T])
    index = np.arange(GROUPS * LOCAL * ROWS)
    g, et, j = np.unravel_index(index, (GROUPS, LOCAL * TRACERS, PLAT))
    final = np.zeros((index.size, index.size), np.float32)
    final[(et * GROUPS + g) * PLAT + j, index] = 1.0
    b = lambda v: np.asarray(v, np.float32).astype(ml_dtypes.bfloat16)
    return (b(forward), b(inverse), b(to_modes), b(to_rows), gain) + (
        b(spread),
        b(gather),
        b(home),
        b(small),
        b(final),
    )


def split_grid(b):
    return b // 16, lax.rem(b // 2, 8), lax.rem(b, 2)


def wrap(value, size):
    return jnp.where(value >= size, value - size, value)


def kernel(
    x_hbm,
    field_hbm,
    fac_hbm,
    cells_hbm,
    measured_hbm,
    variance_hbm,
    forward_hbm,
    inverse_hbm,
    modes_hbm,
    rows_hbm,
    gain_hbm,
    spread_hbm,
    gather_hbm,
    home_hbm,
    small_hbm,
    final_hbm,
    out_hbm,
    mult_out,
    x,
    xb,
    forward,
    inverse,
    modes,
    rows,
    gain,
    spread,
    gather,
    home,
    small,
    final,
    fac_raw,
    cells,
    measured,
    variance,
    field,
    field_rows,
    send1,
    recv1,
    staged,
    plane,
    damped,
    send2,
    recv2,
    padded,
    coefficients,
    fac,
    fac_in,
    fac_wide,
    mix,
    log_mean,
    log_spread,
    log_new,
    background,
    weighted,
    spread_seen,
    projected,
    transform,
    send3,
    recv3,
    result,
    mult_send,
    mult_in,
    load_sem,
    local_sem,
    send_sem,
    recv_sem,
    patch_sem,
    pair_sem,
    ready,
):
    g, b = lax.axis_index("mem"), lax.axis_index("grid")
    half, z, core = split_grid(b)
    member = half * 2 + core

    def load(src, dst, i):
        return pltpu.make_async_copy(src, dst, load_sem.at[i])

    load_x = load(x_hbm, x, 0)
    load_x.start()
    load_fac = [load(fac_hbm, fac_raw, 13), load(small_hbm, small, 14)]
    for one in load_fac:
        one.start()
    load_forward = [load(forward_hbm.at[i], forward.at[i], 1 + i) for i in range(4)]
    for one in load_forward:
        one.start()
    parity = lax.rem(z, 2)
    later = [
        load(modes_hbm.at[parity], modes, 5),
        load(rows_hbm.at[parity], rows, 6),
        load(gain_hbm.at[z], gain, 7),
        load(spread_hbm, spread, 8),
        load(field_hbm, field, 9),
        load(inverse_hbm, inverse, 10),
        load(gather_hbm, gather, 11),
        load(home_hbm, home, 12),
        load(final_hbm, final, 18),
        load(cells_hbm, cells, 15),
        load(measured_hbm, measured, 16),
        load(variance_hbm, variance, 17),
    ]

    barrier = pltpu.get_barrier_semaphore()

    groups = [wrap(g + step, GROUPS) for step in range(1, GROUPS)]
    bands = [
        wrap(half + a, 2) * 16 + wrap(z + dz, BLOCKS) * 2 + wrap(core + c, 2)
        for a, c in PAIRS
        for dz in ZSTEPS
        if a or c or dz
    ]
    for to in groups:
        pl.semaphore_signal(barrier, inc=1, device_id=(to, b), device_id_type=MESH)
    for to in bands:
        pl.semaphore_signal(barrier, inc=1, device_id=(g, to), device_id_type=MESH)

    def remote(src, dst, i, to):
        return pltpu.make_async_remote_copy(
            src_ref=src,
            dst_ref=dst,
            send_sem=send_sem.at[i],
            recv_sem=recv_sem.at[i],
            device_id=to,
            device_id_type=MESH,
        )

    def wait_bytes(ref, sem):
        pltpu.make_async_copy(ref, ref, sem).wait()

    load_x.wait()
    xb[...] = x[...].reshape(LOCAL * TRACERS * BAND, NLON).astype(bf16)
    for one in load_forward:
        one.wait()
    for one in later:
        one.start()

    def forward_step(i, carry):
        value = jnp.dot(xb[...], forward[i], preferred_element_type=f32) * (1.0 / NLON)
        value = value.astype(bf16).reshape(LOCAL, TRACERS * BAND, 256)
        send1[2 * i] = value[:, :, :128]
        send1[2 * i + 1] = value[:, :, 128:]
        return carry

    lax.fori_loop(0, 4, forward_step, 0)
    pl.semaphore_wait(barrier, GROUPS + BANDS - 2)
    for to in groups:
        pl.semaphore_signal(ready, inc=1, device_id=(to, b), device_id_type=MESH)
    for band in bands:
        h2, z2, c2 = split_grid(band)
        remote(send1.at[z2, h2 * 2 + c2], recv1.at[b], 0, (g, band)).start()
    own1 = pltpu.make_async_copy(send1.at[z, member], recv1.at[b], local_sem.at[0])
    own1.start()
    pairs = LOCAL * PATCHES
    for one in load_fac:
        one.wait()
    raw = fac_raw[...].astype(f32).reshape(pairs * GROUPS, REACTIONS).astype(bf16)
    fac[...] = jnp.ones(fac.shape, f32)
    raw = jnp.dot(small[0], raw, preferred_element_type=f32)
    fac[:, :, :REACTIONS] = raw.reshape(GROUPS, pairs, REACTIONS)
    for to in groups:
        remote(fac.at[to], fac_in.at[g], 1, (to, b)).start()
    own_fac = pltpu.make_async_copy(fac.at[g], fac_in.at[g], local_sem.at[1])
    own_fac.start()

    for one in later:
        one.wait()
    padded[...] = jnp.zeros(padded.shape, bf16)

    line_of = lax.broadcasted_iota(jnp.int32, (8, BAND), 0) + g * PLAT
    own_lines = jnp.where(line_of == lax.broadcasted_iota(jnp.int32, (8, BAND), 1), 1.0, 0.0)
    own_lines = own_lines.astype(bf16)

    def widen(r, carry):
        field_rows[r] = jnp.dot(own_lines, field[r], preferred_element_type=f32)
        return carry

    lax.fori_loop(0, REACTIONS, widen, 0)
    own_fac.wait()
    wait_bytes(fac_in.at[pl.ds(0, GROUPS - 1)], recv_sem.at[1])
    wait_bytes(fac.at[pl.ds(0, GROUPS - 1)], send_sem.at[1])
    factors = jnp.dot(
        small[1],
        fac_in[...].reshape(GROUPS * pairs, 128).astype(bf16),
        preferred_element_type=f32,
    )
    for c in range(PATCHES):
        for r in range(REACTIONS):
            column = factors[c * MEMBERS : (c + 1) * MEMBERS, r : r + 1]
            fac_wide[c, r] = jnp.broadcast_to(column, (MEMBERS, 128))
    log_rate = jnp.log(factors).reshape(PATCHES, MEMBERS, 128)
    log_mean[...] = jnp.broadcast_to(
        jnp.mean(log_rate, axis=1, keepdims=True), (PATCHES, MEMBERS, 128)
    )
    log_spread[...] = log_rate - log_mean[...]

    own1.wait()
    wait_bytes(recv1.at[pl.ds(0, BANDS - 1)], recv_sem.at[0])

    def unpack(s, carry):
        value = recv1[s].astype(f32)
        at = pl.ds(pl.multiple_of(s * BAND, 8), BAND)
        for t in range(TRACERS):
            staged[at, t * 128 : (t + 1) * 128] = value[t * BAND : (t + 1) * BAND]
        return carry

    lax.fori_loop(0, BANDS, unpack, 0)
    plane[...] = staged[...].astype(bf16)

    def to_modes(i, carry):
        at = pl.ds(pl.multiple_of(i * 128, 128), 128)
        value = jnp.dot(modes[at, :], plane[...], preferred_element_type=f32)
        scale = gain[at, :]
        for t in range(TRACERS):
            lanes = slice(t * 128, (t + 1) * 128)
            damped[at, lanes] = (value[:, lanes] * scale).astype(bf16)
        return carry

    lax.fori_loop(0, NW // 128, to_modes, 0)

    def to_owner(step, carry):
        owner = wrap(g + step, GROUPS)
        at = pl.ds(pl.multiple_of(owner * 96, 32), 96)
        value = jnp.dot(rows[at, :], damped[...], preferred_element_type=f32).astype(bf16)
        stacked = jnp.concatenate([value[:, t * 128 : (t + 1) * 128] for t in range(TRACERS)], 0)
        wide = jnp.dot(spread[...], stacked, preferred_element_type=f32)
        wide = wide.reshape(BANDS, 16, 128).astype(bf16)
        send2[pl.ds(owner * BANDS, BANDS)] = wide[:, :ROWS]
        push(step, owner, 0)
        return carry

    def push(step, owner, to_core):
        for a in (1, 0):
            for dz in ZSTEPS:
                band = wrap(half + a, 2) * 16 + wrap(z + dz, BLOCKS) * 2 + to_core
                copy = pltpu.make_async_remote_copy(
                    src_ref=send2.at[owner * BANDS + band],
                    dst_ref=recv2.at[g, half, z, core],
                    send_sem=send_sem.at[2],
                    recv_sem=pair_sem.at[z // 2],
                    device_id=(owner, band),
                    device_id_type=MESH,
                )
                if a or dz:
                    copy.start()
                else:
                    pl.when(jnp.logical_or(step != 0, core != to_core))(copy.start)

    def push_rest(step, carry):
        push(step, wrap(g + step, GROUPS), 1)
        return carry

    def reaction_step(c, carry):
        for j in range(PLAT):
            for h in range(PLON // 128):
                lanes = pl.ds(pl.multiple_of(c * PLON + h * 128, 128), 128)
                rates = [fac_wide[c, r] * field_rows[r, j : j + 1, lanes] for r in range(REACTIONS)]
                for s in range(TRACERS):
                    outflow = rates[3 * s] + rates[3 * s + 1] + rates[3 * s + 2]
                    leave = 1.0 / (1.0 + outflow)
                    mix[c, j, h, s, s] = leave
                    for t in range(TRACERS):
                        if t != s:
                            mix[c, j, h, t, s] = rates[3 * s + (t if t < s else t - 1)] * leave
        return carry

    pl.semaphore_wait(ready, GROUPS - 1)
    lax.fori_loop(0, GROUPS, to_owner, 0)
    lax.fori_loop(0, GROUPS, push_rest, 0)
    own2 = pltpu.make_async_copy(
        send2.at[g * BANDS + b], recv2.at[g, half, z, core], pair_sem.at[z // 2]
    )
    own2.start()
    lax.fori_loop(0, PATCHES, reaction_step, 0)

    for i in range(BLOCKS // 2):
        wait_bytes(recv2.at[:, :, pl.ds(2 * i, 2)], pair_sem.at[i])
        for block in (2 * i, 2 * i + 1):
            value = recv2[:, :, block, :, :, :].reshape(MEMBERS, ROWS, 128)
            padded[:, :ROWS, block * 128 : (block + 1) * 128] = value
        lanes = slice(i * 256, (i + 1) * 256)
        value = padded[:, :, lanes].reshape(MEMBERS * 16, 256)
        coefficients[:, lanes] = jnp.dot(
            gather[...], value, preferred_element_type=f32
        ).astype(bf16)

    obs = cells.shape[-1]

    def background_step(c):
        smooth = jnp.dot(coefficients[...], inverse[c], preferred_element_type=f32)
        smooth = smooth.reshape(TRACERS, PLAT, MEMBERS, PLON)
        for j in range(PLAT):
            for h in range(PLON // 128):
                tracers = [smooth[t, j, :, h * 128 : (h + 1) * 128] for t in range(TRACERS)]
                for t in range(TRACERS):
                    value = mix[c, j, h, t, t] * tracers[t]
                    for s in range(TRACERS):
                        if s != t:
                            value = value + mix[c, j, h, t, s] * tracers[s]
                    row = (t * PLAT + j) * MEMBERS
                    background[c, row : row + MEMBERS, h * 128 : (h + 1) * 128] = value.astype(
                        bf16
                    )
        cell = cells[c, pl.ds(g, 1), :]
        column = jnp.bitwise_and(cell, PLON - 1)
        row = lax.shift_right_logical(cell, 8)
        picker = jnp.where(
            lax.broadcasted_iota(jnp.int32, (PLON, obs), 0) == column, 1.0, 0.0
        ).astype(bf16)
        seen = jnp.dot(background[c], picker, preferred_element_type=f32)
        predicted = jnp.zeros((MEMBERS, obs), f32)
        for k in range(ROWS):
            predicted = predicted + jnp.where(
                row == k, seen[k * MEMBERS : (k + 1) * MEMBERS], 0.0
            )
        seen_mean = jnp.mean(predicted, axis=0, keepdims=True)
        spread_of = predicted - seen_mean
        weight = spread_of * (1.0 / variance[c, pl.ds(g, 1), :])
        innovation = measured[c, pl.ds(g, 1), :] - seen_mean
        at = pl.ds(c * MEMBERS, MEMBERS)
        weighted[at, :] = weight
        spread_seen[at, :] = spread_of
        projected[at, :] = jnp.broadcast_to(
            jnp.sum(weight * innovation, axis=1, keepdims=True), (MEMBERS, 128)
        )

    def halves(value):
        high = value.astype(bf16)
        return high, (value - high.astype(f32)).astype(bf16)

    def exact(left, right):
        (a, b), (c, d) = halves(left), halves(right)
        dot = functools.partial(jnp.dot, preferred_element_type=f32)
        return dot(a, c) + (dot(a, d) + dot(b, c))

    def solve(first, last):
        size = (last - first) * MEMBERS
        at = slice(first * MEMBERS, last * MEMBERS)
        block_row = lax.broadcasted_iota(jnp.int32, (size, size), 0)
        block_col = lax.broadcasted_iota(jnp.int32, (size, size), 1)
        same = block_row // MEMBERS == block_col // MEMBERS
        identity = jnp.where(block_row == block_col, 1.0, 0.0)
        outer = lax.dot_general(
            weighted[at, :],
            spread_seen[at, :],
            (((1,), (1,)), ((), ())),
            precision=HI,
            preferred_element_type=f32,
        )
        outer = jnp.where(same, outer, 0.0)
        square = jnp.sum(outer * outer, axis=1, keepdims=True).reshape(last - first, MEMBERS, 1)
        square = jnp.broadcast_to(jnp.sum(square, axis=1, keepdims=True), (last - first, MEMBERS, 1))
        scale = (MEMBERS - 1.0) + jnp.sqrt(square.reshape(size, 1))
        current = ((MEMBERS - 1.0) * identity + outer) / scale
        root = 1.5 * identity - 0.5 * current
        current = exact(current, root)
        for sweep in range(1, SWEEPS):
            middle = 1.5 * identity - 0.5 * exact(root, current)
            if sweep < SWEEPS - 1:
                current = exact(current, middle)
            root = exact(middle, root)
        mean_weight = exact(root, exact(root, projected[at, :])) / scale
        full = jnp.where(same, jnp.sqrt((MEMBERS - 1.0) / scale) * root, 0.0)
        fold = jnp.where(
            lax.rem(lax.broadcasted_iota(jnp.int32, (size, MEMBERS), 0), MEMBERS)
            == lax.broadcasted_iota(jnp.int32, (size, MEMBERS), 1),
            1.0,
            0.0,
        )
        transform[at, :] = exact(full, fold) + mean_weight[:, :MEMBERS]

    def apply(matrix, values, precision=None):
        return lax.dot_general(
            matrix,
            values,
            (((0,), (0,)), ((), ())),
            precision=precision,
            preferred_element_type=f32,
        )

    def analysis_step(c):
        matrix = transform[c * MEMBERS : (c + 1) * MEMBERS, :]
        pieces = []
        for k in range(ROWS):
            value = background[c, k * MEMBERS : (k + 1) * MEMBERS, :].astype(f32)
            center = jnp.mean(value, axis=0, keepdims=True)
            pieces.append((center + apply(matrix, value - center)).astype(bf16))
        analysed = jnp.concatenate(pieces, axis=0)
        sent = jnp.dot(home[...], analysed, preferred_element_type=f32).astype(bf16)
        send3[c] = sent.reshape(GROUPS, LOCAL * ROWS, PLON)
        for to in groups:
            pltpu.make_async_remote_copy(
                src_ref=send3.at[c, to],
                dst_ref=recv3.at[c, g],
                send_sem=send_sem.at[3],
                recv_sem=patch_sem.at[c],
                device_id=(to, b),
                device_id_type=MESH,
            ).start()
        recv3[c, g] = send3[c, g]

    def multipliers(c):
        matrix = transform[c * MEMBERS : (c + 1) * MEMBERS, :]
        log_new[c] = jnp.exp(log_mean[c] + apply(matrix, log_spread[c], HI))

    def finish(first, last):
        for c in range(first, last):
            multipliers(c)
        if last == PATCHES:
            send_multipliers()
        for c in range(first, last):
            analysis_step(c)

    own_mult = pltpu.make_async_copy(mult_send.at[g], mult_in.at[g], local_sem.at[4])

    def send_multipliers():
        mult = log_new[...].reshape(PATCHES * MEMBERS, 128).astype(bf16)
        mult = jnp.dot(small[2], mult, preferred_element_type=f32)
        mult_send[...] = mult.reshape(GROUPS, pairs, 128)
        for to in groups:
            remote(mult_send.at[to], mult_in.at[g], 4, (to, b)).start()
        own_mult.start()

    first = 0
    for count in TOGETHER:
        last = first + count
        for c in range(first, last):
            background_step(c)
        if first:
            finish(before, first)
        solve(first, last)
        before, first = first, last
    finish(before, first)

    def store(c):
        lanes = pl.ds(c * PLON if isinstance(c, int) else pl.multiple_of(c * PLON, PLON), PLON)
        return pltpu.make_async_copy(result.at[:, lanes], out_hbm.at[:, lanes], local_sem.at[3])

    def final_step(c, carry):
        wait_bytes(recv3.at[c, pl.ds(0, GROUPS - 1)], patch_sem.at[c])
        lanes = pl.ds(c * PLON if isinstance(c, int) else pl.multiple_of(c * PLON, PLON), PLON)
        value = recv3[c].reshape(GROUPS * LOCAL * ROWS, PLON)
        result[:, lanes] = jnp.dot(final[...], value, preferred_element_type=f32).astype(bf16)
        store(c).start()
        return carry

    lax.fori_loop(0, PATCHES - 1, final_step, 0)
    own_mult.wait()
    wait_bytes(mult_in.at[pl.ds(0, GROUPS - 1)], recv_sem.at[4])
    mult = mult_in[...].reshape(GROUPS * pairs, 128).astype(bf16)
    mult = jnp.dot(small[3], mult, preferred_element_type=f32)
    mult_out[...] = mult.reshape(LOCAL, PATCHES, GROUPS, 128)[..., :REACTIONS].astype(bf16)
    final_step(PATCHES - 1, 0)
    wait_bytes(result, local_sem.at[3])
    wait_bytes(send1.at[pl.ds(0, BLOCKS - 1)], send_sem.at[0])
    wait_bytes(send1.at[0, pl.ds(0, LOCAL - 1)], send_sem.at[0])
    wait_bytes(send2.at[pl.ds(0, GROUPS * BANDS - 1)], send_sem.at[2])
    wait_bytes(send3.at[:, pl.ds(0, GROUPS - 1)], send_sem.at[3])
    wait_bytes(mult_send.at[pl.ds(0, GROUPS - 1)], send_sem.at[4])


def keep(values, mult, out, mult_out, held, mult_held, in_sem, out_sem):
    pieces = [(mult, mult_held, mult_out)]
    for i in range(8):
        at = pl.ds(i * 48, 48)
        pieces.append((values.at[at], held.at[at], out.at[at]))
    reads = [pltpu.make_async_copy(a, b, in_sem.at[i]) for i, (a, b, _) in enumerate(pieces)]
    writes = [pltpu.make_async_copy(b, c, out_sem.at[i]) for i, (_, b, c) in enumerate(pieces)]
    for read in reads:
        read.start()
    for read, write in zip(reads, writes):
        read.wait()
        write.start()
    for write in writes:
        write.wait()


def on_device(x, field, kinetic, cells, measured, variance):
    constants = tables()
    anywhere = pl.BlockSpec(memory_space=pl.ANY)
    vmem = pl.BlockSpec(memory_space=pltpu.VMEM)
    size = PATCHES * MEMBERS
    pairs = LOCAL * PATCHES
    obs = cells.shape[-1]
    scratch = [
        pltpu.VMEM((LOCAL, TRACERS, BAND, NLON), f32),
        pltpu.VMEM((LOCAL * TRACERS * BAND, NLON), bf16),
        pltpu.VMEM((4, NLON, 256), bf16),
        pltpu.VMEM((PATCHES, 2 * NW, PLON), bf16),
        pltpu.VMEM((NW, NLAT), bf16),
        pltpu.VMEM((NLAT, NW), bf16),
        pltpu.VMEM((NW, 128), f32),
        pltpu.VMEM(constants[5].shape, bf16),
        pltpu.VMEM(constants[6].shape, bf16),
        pltpu.VMEM(constants[7].shape, bf16),
        pltpu.VMEM(constants[8].shape, bf16),
        pltpu.VMEM(constants[9].shape, bf16),
        pltpu.VMEM((LOCAL, PATCHES, GROUPS, REACTIONS), bf16),
        pltpu.VMEM((PATCHES, GROUPS, obs), jnp.int32),
        pltpu.VMEM((PATCHES, GROUPS, obs), f32),
        pltpu.VMEM((PATCHES, GROUPS, obs), f32),
        pltpu.VMEM((REACTIONS, BAND, NLON), bf16),
        pltpu.VMEM((REACTIONS, 8, NLON), f32),
        pltpu.VMEM((BLOCKS, LOCAL, TRACERS * BAND, 128), bf16),
        pltpu.VMEM((BANDS, TRACERS * BAND, 128), bf16),
        pltpu.VMEM((NLAT, TRACERS * 128), f32),
        pltpu.VMEM((NLAT, TRACERS * 128), bf16),
        pltpu.VMEM((NW, TRACERS * 128), bf16),
        pltpu.VMEM((GROUPS * BANDS, ROWS, 128), bf16),
        pltpu.VMEM((GROUPS, 2, BLOCKS, 2, ROWS, 128), bf16),
        pltpu.VMEM((MEMBERS, 16, BLOCKS * 128), bf16),
        pltpu.VMEM((ROWS * MEMBERS, 2 * NW), bf16),
        pltpu.VMEM((GROUPS, pairs, 128), f32),
        pltpu.VMEM((GROUPS, pairs, 128), f32),
        pltpu.VMEM((PATCHES, REACTIONS, MEMBERS, 128), f32),
        pltpu.VMEM((PATCHES, PLAT, 2, TRACERS, TRACERS, MEMBERS, 128), f32),
        pltpu.VMEM((PATCHES, MEMBERS, 128), f32),
        pltpu.VMEM((PATCHES, MEMBERS, 128), f32),
        pltpu.VMEM((PATCHES, MEMBERS, 128), f32),
        pltpu.VMEM((PATCHES, ROWS * MEMBERS, PLON), bf16),
        pltpu.VMEM((size, 128), f32),
        pltpu.VMEM((size, 128), f32),
        pltpu.VMEM((size, 128), f32),
        pltpu.VMEM((size, MEMBERS), f32),
        pltpu.VMEM((PATCHES, GROUPS, LOCAL * ROWS, PLON), bf16),
        pltpu.VMEM((PATCHES, GROUPS, LOCAL * ROWS, PLON), bf16),
        pltpu.VMEM((LOCAL * TRACERS * BAND, NLON), bf16),
        pltpu.VMEM((GROUPS, pairs, 128), f32),
        pltpu.VMEM((GROUPS, pairs, 128), f32),
        pltpu.SemaphoreType.DMA((19,)),
        pltpu.SemaphoreType.DMA((5,)),
        pltpu.SemaphoreType.DMA((5,)),
        pltpu.SemaphoreType.DMA((5,)),
        pltpu.SemaphoreType.DMA((PATCHES,)),
        pltpu.SemaphoreType.DMA((BLOCKS // 2,)),
        pltpu.SemaphoreType.REGULAR,
    ]
    out, mult = pl.pallas_call(
        kernel,
        out_shape=(
            jax.ShapeDtypeStruct((LOCAL * TRACERS * BAND, NLON), bf16),
            jax.ShapeDtypeStruct((LOCAL, PATCHES, GROUPS, REACTIONS), bf16),
        ),
        in_specs=[anywhere] * (6 + len(constants)),
        out_specs=(anywhere, vmem),
        scratch_shapes=scratch,
        compiler_params=pltpu.CompilerParams(
            collective_id=0, has_side_effects=True, vmem_limit_bytes=60 << 20
        ),
        name="assimilate",
    )(
        x,
        field,
        kinetic.transpose(0, 3, 2, 1),
        cells.transpose(1, 0, 2),
        measured.transpose(1, 0, 2),
        variance.transpose(1, 0, 2),
        *constants,
    )
    out, mult = pl.pallas_call(
        keep,
        out_shape=(
            jax.ShapeDtypeStruct(out.shape, bf16),
            jax.ShapeDtypeStruct(mult.shape, bf16),
        ),
        in_specs=[anywhere] * 2,
        out_specs=(anywhere,) * 2,
        scratch_shapes=[
            pltpu.VMEM(out.shape, bf16),
            pltpu.VMEM(mult.shape, bf16),
            pltpu.SemaphoreType.DMA((9,)),
            pltpu.SemaphoreType.DMA((9,)),
        ],
        compiler_params=pltpu.CompilerParams(vmem_limit_bytes=60 << 20),
        name="keep",
    )(out, mult)
    return out.reshape(LOCAL, TRACERS, BAND, NLON), mult.transpose(0, 3, 2, 1)


def solution(mesh):
    return jax.shard_map(
        on_device,
        mesh=mesh,
        in_specs=(
            P("mem", None, "grid", None),
            P(None, "grid", None),
            P("mem", None, "grid", None),
            P("grid", None, None),
            P("grid", None, None),
            P("grid", None, None),
        ),
        out_specs=(P("mem", None, "grid", None), P("mem", None, "grid", None)),
        check_vma=False,
    )
```
